32 devices in a mesh: groups: 2 (over x), seq: 16 (over z, y, core).
Axes of the slice: x: 2, y: 2, z: 4, core: 2. Of those that a mesh axis runs over, the one named last changes fastest.
Arguments:
- features: bfloat16 [4, 8192, 768], P('groups', 'seq'), parts along dimension 0, may hold values from -6 to 6
- gain_first: float32 [768], replicated, may hold values from 0.1 to 1.9
- kernel_first: float32 [5, 768], replicated, may hold values from -2.5 to 2.5
- weight_first: bfloat16 [768, 768], replicated, may hold values from -0.21875 to 0.21875
- bias_first: float32 [768], replicated, may hold values from -3 to 3
- gain_second: float32 [768], replicated, may hold values from 0.1 to 1.9
- kernel_second: float32 [5, 768], replicated, may hold values from -2.5 to 2.5
- weight_second: bfloat16 [768, 896], replicated, may hold values from -0.21875 to 0.21875
- bias_second: float32 [896], replicated, may hold values from -3 to 3
- cotangent: bfloat16 [4, 2048, 896], P('groups', 'seq'), parts along dimension 0, may hold values from -6 to 6
Outputs:
- grad_features: bfloat16 [4, 8192, 768], P('groups', 'seq'), parts along dimension 0
- grad_weight_first: float32 [1536, 768], P('groups', 'seq'), parts along dimension 0
- grad_weight_second: float32 [1536, 896], P('groups', 'seq'), parts along dimension 0
- grad_bias_first: float32 [1536], P('groups'), parts along dimension 0
- grad_bias_second: float32 [1792], P('groups'), parts along dimension 0
- grad_kernel_first: float32 [10, 768], P('groups'), parts along dimension 0
- grad_kernel_second: float32 [10, 768], P('groups'), parts along dimension 0
- grad_gain_first: float32 [1536], P('groups'), parts along dimension 0
- grad_gain_second: float32 [1536], P('groups'), parts along dimension 0
The draws below stay inside these ranges and needn't reach their ends.
There are 2 independent parts, one for each index of `groups`. The reference program is written for one: setup_inputs(seed, part) draws one part's arguments, and reference() takes and returns one part's arrays. A program takes and returns all parts, laid end to end along the dimension named above; an argument that names none is the same for every part. Nothing has to cross between parts.
All inputs are finite; a program needn't handle non-finite values.
Results may differ from the reference program's by a relative error of at most 0.0067.
Values may be sent and summed in bfloat16 or wider, within the bound.
A program may use at most 128 MiB of HBM per device.

```python
import math
import jax
import jax.numpy as jnp
from jax import lax

C1 = 768
C2 = 896
TAPS = 5
BATCH = 2
LENGTH = 8192


def spiked(entries, own_key, source, target, blocks, factor):
    owner, partner = [(jnp.arange(entries.shape[position]) // (entries.shape[position] // blocks)).reshape([-1 if axis == position else 1 for axis in range(entries.ndim)]) for position in (source, target)]
    chosen = jax.random.permutation(own_key, blocks)[partner]
    strong = (owner == chosen) | (owner == (partner + blocks // 2) % blocks)
    return jnp.where(strong, factor * entries, entries)


def levels(key, shape, shards, least, largest):
    gain = 1.0
    for dim, shards_of in shards:
        steps = jax.random.uniform(jax.random.fold_in(jax.random.fold_in(key, 6), dim), (shards_of,), jnp.float32, least / len(shards), largest / len(shards))
        gain = gain * jnp.repeat(jnp.exp(steps), shape[dim] // shards_of).reshape((-1,) + (1,) * (len(shape) - 1 - dim))
    return gain


def bell_draw(key, dims, scale, most, pieces=(), kind=jnp.bfloat16):
    result = jax.random.normal(key, dims, jnp.float32) * scale
    if len(pieces) > 0:
        result = levels(key, dims, pieces, -0.22, 0.18) * result
    return jnp.clip(result, min=-most, max=most).astype(kind)


def bell_draw_with(stream_key, dims, deviation, most, cuts, heavy, kind=jnp.bfloat16):
    result = deviation * jax.random.normal(stream_key, dims, jnp.float32)
    if cuts:
        result = result * levels(stream_key, dims, cuts, -0.22, 0.18)
    return jnp.clip(spiked(result, jax.random.fold_in(stream_key, 3), *heavy), -most, most).astype(kind)


def setup_inputs(seed: int = 0, part: int = 0) -> dict:
    key_of = jax.random.split(jax.random.key(seed), 11)
    own_keys = jax.random.split(jax.random.fold_in(key_of[10], part), 11)
    return {
        "features": bell_draw(own_keys[0], (BATCH, LENGTH, C1), 1.0, 6.0, ((1, 16),)),
        "gain_first": jnp.clip(1.0 + 0.18 * jax.random.normal(key_of[1], (C1,), jnp.float32), 0.1, 1.9),
        "kernel_first": bell_draw(key_of[2], (TAPS, C1), TAPS ** -0.5, 2.5, (), jnp.float32),
        "weight_first": bell_draw(key_of[3], (C1, C1), C1 ** -0.5, 0.21875),
        "bias_first": bell_draw(key_of[4], (C1,), 0.5, 3.0, (), jnp.float32),
        "gain_second": jnp.clip(1.0 + 0.18 * jax.random.normal(key_of[5], (C1,), jnp.float32), 0.1, 1.9),
        "kernel_second": bell_draw(key_of[6], (TAPS, C1), TAPS ** -0.5, 2.5, (), jnp.float32),
        "weight_second": bell_draw(key_of[7], (C1, C2), C1 ** -0.5, 0.21875),
        "bias_second": bell_draw(key_of[8], (C2,), 0.5, 3.0, (), jnp.float32),
        "cotangent": bell_draw_with(own_keys[9], (BATCH, LENGTH // 4, C2), 1.0, 6.0, ((1, 16),), (1, 2, 16, 2.0)),
    }


epsilon = 1e-06
inv_sqrt_two = 0.7071067811865476
inv_sqrt_tau = 0.3989422804014327

def gelu_pair(inputs):
    normal_cdf = 0.5 * (1.0 + jax.scipy.special.erf(inputs * inv_sqrt_two))
    density = jnp.exp(-0.5 * inputs * inputs) * inv_sqrt_tau
    return (inputs * normal_cdf, normal_cdf + inputs * density)

def rms_forward(values, gain_vec):
    factor = lax.rsqrt(lax.optimization_barrier(jnp.mean(values * values, axis=-1, keepdims=True)) + epsilon)
    return (values * factor * gain_vec, factor)

def rms_backward(values, factor, gain_vec, grad_norm):
    scaled = grad_norm * gain_vec
    inner = lax.optimization_barrier(jnp.mean(scaled * values, axis=-1, keepdims=True))
    return factor * scaled - values * (factor * factor * factor) * inner

def pad_two(values):
    return jnp.pad(values, ((0, 0), (2, 2), (0, 0)))

def taps_forward(padded, kernel, extent):
    total = kernel[0] * padded[:, 0:extent]
    for offset in range(1, 5):
        total = total + kernel[offset] * padded[:, offset:offset + extent]
    return total

def taps_backward(padded, kernel, extent):
    total = kernel[0] * padded[:, 4:4 + extent]
    for offset in range(1, 5):
        total = total + kernel[offset] * padded[:, 4 - offset:4 - offset + extent]
    return total

def taps_kernel(padded, grad_conv, extent):
    return jnp.stack([lax.optimization_barrier(jnp.sum(padded[:, offset:offset + extent] * grad_conv, axis=(0, 1))) for offset in range(5)])

def project(matrix, weight):
    flat = matrix.reshape(-1, matrix.shape[-1])
    return jnp.dot(flat, weight, preferred_element_type=jnp.float32).reshape(matrix.shape[0], matrix.shape[1], weight.shape[1])

def project_back(matrix, weight):
    flat = matrix.reshape(-1, matrix.shape[-1])
    return jnp.dot(flat, weight.T, preferred_element_type=jnp.float32).reshape(matrix.shape[0], matrix.shape[1], weight.shape[0])

def weight_grad(matrix, other):
    flat_left = matrix.reshape(-1, matrix.shape[-1])
    flat_right = other.reshape(-1, other.shape[-1])
    return lax.dot_general(flat_left, flat_right, (((0,), (0,)), ((), ())), preferred_element_type=jnp.float32)

def pool_pairs(values):
    return (values[:, 0::2] + values[:, 1::2]) * 0.5

def spread_pairs(values):
    return jnp.repeat(values * 0.5, 2, axis=1)

def widen(values):
    return lax.optimization_barrier(values.astype(jnp.bfloat16)).astype(jnp.float32)

def reference(features, gain_first, kernel_first, weight_first, bias_first, gain_second, kernel_second, weight_second, bias_second, cotangent):
    channels = features.shape[2]
    extent = features.shape[1]
    pooled_len = extent // 2
    norm_scale = 1.0 / math.sqrt(features.shape[0] * extent)
    values = features.astype(jnp.float32)
    norm_first, factor_first = rms_forward(values, gain_first)
    norm_first_pad = pad_two(norm_first)
    conv_first = taps_forward(norm_first_pad, kernel_first, extent).astype(jnp.bfloat16)
    pre_first = project(conv_first, weight_first) + bias_first
    act_first, slope_first = gelu_pair(pre_first)
    pooled = pool_pairs(values + act_first).astype(jnp.bfloat16)
    pooled_f = pooled.astype(jnp.float32)
    norm_second, factor_second = rms_forward(pooled_f, gain_second)
    norm_second_pad = pad_two(norm_second)
    conv_second = taps_forward(norm_second_pad, kernel_second, pooled_len).astype(jnp.bfloat16)
    pre_second = project(conv_second, weight_second) + bias_second
    unused, slope_second = gelu_pair(pre_second)
    up_second = spread_pairs(cotangent.astype(jnp.float32))
    back_second = (up_second * slope_second).astype(jnp.bfloat16)
    grad_weight_second = weight_grad(conv_second, back_second) * norm_scale
    grad_bias_second = lax.optimization_barrier(jnp.sum(back_second.astype(jnp.float32), axis=(0, 1))) * norm_scale
    into_second = widen(project_back(back_second, weight_second))
    dnorm_second = taps_backward(pad_two(into_second), kernel_second, pooled_len)
    grad_kernel_second = taps_kernel(norm_second_pad, into_second, pooled_len) * norm_scale
    grad_gain_second = lax.optimization_barrier(jnp.sum(dnorm_second * pooled_f * factor_second, axis=(0, 1))) * norm_scale
    dpooled = rms_backward(pooled_f, factor_second, gain_second, dnorm_second) + up_second[:, :, :channels]
    up_first = spread_pairs(dpooled)
    back_first = (up_first * slope_first).astype(jnp.bfloat16)
    grad_weight_first = weight_grad(conv_first, back_first) * norm_scale
    grad_bias_first = lax.optimization_barrier(jnp.sum(back_first.astype(jnp.float32), axis=(0, 1))) * norm_scale
    into_first = widen(project_back(back_first, weight_first))
    dnorm_first = taps_backward(pad_two(into_first), kernel_first, extent)
    grad_kernel_first = taps_kernel(norm_first_pad, into_first, extent) * norm_scale
    grad_gain_first = lax.optimization_barrier(jnp.sum(dnorm_first * values * factor_first, axis=(0, 1))) * norm_scale
    grad_features = (up_first + rms_backward(values, factor_first, gain_first, dnorm_first)).astype(jnp.bfloat16)
    return (grad_features, grad_weight_first, grad_weight_second, grad_bias_first, grad_bias_second, grad_kernel_first, grad_kernel_second, grad_gain_first, grad_gain_second)
```

```python
import functools
import math

import jax
import jax.numpy as jnp
from jax import lax
from jax.experimental import pallas as pl
from jax.experimental.pallas import tpu as pltpu
from jax.sharding import PartitionSpec as P

MESH = pl.DeviceIdType.MESH
F32 = jnp.float32
BF16 = jnp.bfloat16
epsilon = 1e-06
inv_sqrt_two = 0.7071067811865476
inv_sqrt_tau = 0.3989422804014327
HALO = 16
LANES = 128


def gelu_parts(v):
    cdf = 0.5 * (1.0 + lax.erf(v * inv_sqrt_two))
    return cdf, jnp.exp(-0.5 * v * v) * inv_sqrt_tau


def step_kernel(
    scale,
    n,
    blocks,
    x_hbm,
    g1_in,
    k1_ref,
    w1_hbm,
    b1_in,
    g2_in,
    k2_ref,
    w2_hbm,
    b2_in,
    c_hbm,
    out_hbm,
    *rest,
):
    if blocks:
        sum1_ref, sum2_ref, small_out = rest[:3]
    else:
        gt1_ref, gt2_ref, small_out = rest[:3]
    (x_ref, c_ref, xs, xp, fac, fac_own, conv, slope, up, fac2, fac2_own, conv2, conv2_own, back2,
     into2, cot, ss, own, inside, back, into, dn, gt, mix, fin, xb_ref, xa_ref, cb_ref, ca_ref,
     w1_ref, w2_ref, g1_ref, b1_ref, g2_ref, b2_ref, small_ref, halo_send, halo_recv, load_sem,
     out_sem) = rest[3:43]
    rest = rest[43:]
    batch, length, ch = x_ref.shape
    ch2 = c_ref.shape[2]
    span = length + 2 * HALO
    per = span // 4
    rows = batch * per
    groups = ch // LANES
    side = HALO // 4
    wide = 256
    pitch = rows + 16
    block = 16
    edges = [i for i in range(0, rows, block) if any((i + j) % per in (0, per - 1) for j in range(block))]

    def plane(r, i=0, size=None):
        first = r * pitch + 8 + i
        return slice(first, first + (rows if size is None else size))

    me = lax.axis_index("seq")
    right, left = lax.rem(me + 1, n), lax.rem(me + n - 1, n)
    others = [left, right]
    if blocks:
        z, y, core = me // 4, lax.rem(me // 2, 2), lax.rem(me, 2)
        mate, over = me + 1 - 2 * core, me + 2 - 4 * y
        near = z + 1 - 2 * lax.rem(z, 2)
        order = [lax.rem(z + 2, 4), lax.rem(near + 2, 4), near, z]

        def at_z(zt):
            return zt * 4 + y * 2 + core

        others += [mate, over] + [at_z(zt) for zt in order[:3]]
    loads = [
        pltpu.make_async_copy(source, target, load_sem.at[k])
        for k, (source, target) in enumerate(
            ((x_hbm, x_ref), (c_hbm, c_ref), (w1_hbm, w1_ref), (w2_hbm, w2_ref))
        )
    ]
    barrier = pltpu.get_barrier_semaphore()
    for other in others:
        pl.semaphore_signal(barrier, inc=1, device_id={"seq": other}, device_id_type=MESH)
    for load in loads:
        load.start()
    for source, target in ((g1_in, g1_ref), (b1_in, b1_ref), (g2_in, g2_ref), (b2_in, b2_ref)):
        target[...] = source[...].reshape(target.shape)

    within = lax.broadcasted_iota(jnp.int32, (rows, LANES), 0)
    for b in range(1, batch):
        within = jnp.where(within >= per, within - per, within)
    is_own = (within >= side) & (within < per - side)
    own[...] = jnp.where(is_own, 1.0, 0.0)
    at_first, at_last = me == 0, me == n - 1
    low = jnp.where(at_first, side, 0)
    high = jnp.where(at_last, per - side, per)
    inside[...] = jnp.where((within >= low) & (within < high), 1.0, 0.0)
    small_ref[...] = jnp.zeros_like(small_ref)
    for ref, m in ((fac, 4), (fac_own, 4), (fac2, 2), (fac2_own, 2)):
        for r in range(m):
            for i in (-8, rows):
                ref[plane(r, i, 8)] = jnp.zeros((8, LANES), F32)
    for ref, m in ((xp, 4), (into, 4), (up, 2), (into2, 2)):
        for r in range(m):
            for i in (-8, rows):
                ref[:, plane(r, i, 8)] = jnp.zeros((groups, 8, LANES), F32)
    pl.semaphore_wait(barrier, len(others))

    def remote(source, target, sems, k, other):
        if not isinstance(k, tuple):
            k = (k, k)
        return pltpu.make_async_remote_copy(
            src_ref=source,
            dst_ref=target,
            send_sem=sems[0].at[k[0]],
            recv_sem=sems[1].at[k[1]],
            device_id={"seq": other},
            device_id_type=MESH,
        )

    def send(*args):
        copy = remote(*args)
        copy.start()
        return copy

    halo = []
    for ref, before, after in ((x_hbm, xb_ref, xa_ref), (c_hbm, cb_ref, ca_ref)):
        last = ref.shape[1] - HALO
        for source, target, other in (
            (ref.at[:, pl.ds(last, HALO)], before, right),
            (ref.at[:, pl.ds(0, HALO)], after, left),
        ):
            halo.append(send(source, target, (halo_send, halo_recv), len(halo), other))

    def lanes(c, width=LANES):
        if isinstance(c, int):
            return slice(c * width, (c + 1) * width)
        return pl.ds(pl.multiple_of(c * width, width), width)

    loads[0].wait()

    @pl.loop(0, groups)
    def _(c):
        for b in range(batch):
            base = b * span + HALO
            xs[c, base : base + length] = x_ref[b, :, lanes(c)].astype(F32)

    loads[1].wait()
    for b in range(batch):
        cot[b * per + side : (b + 1) * per - side] = c_ref[b].astype(F32) * 0.5
    for copy in halo:
        copy.wait()

    for b in range(batch):
        base = b * per
        first = cb_ref[b].astype(F32)[HALO - side :] * 0.5
        last = ca_ref[b].astype(F32)[:side] * 0.5
        cot[base : base + side] = jnp.where(at_first, 0.0, first)
        cot[base + per - side : base + per] = jnp.where(at_last, 0.0, last)

    for c in range(groups):
        for b in range(batch):
            base = b * span
            xs[c, base : base + HALO] = jnp.where(at_first, 0.0, xb_ref[b, :, lanes(c)].astype(F32))
            xs[c, base + HALO + length : base + span] = jnp.where(
                at_last, 0.0, xa_ref[b, :, lanes(c)].astype(F32)
            )

    def factor(total):
        return jnp.broadcast_to(
            lax.rsqrt(jnp.sum(total, axis=1, keepdims=True) * (1.0 / ch) + epsilon), total.shape
        )

    @pl.loop(0, batch)
    def _(b):
        for i in range(0, per, 8):
            for r in range(4):
                at = pl.ds(pl.multiple_of(b * per + (r * pitch + 8 + i), 8), 8)
                total = None
                for c in range(groups):
                    v = xs[c, pl.ds(b * span + (4 * i + r), 8, stride=4), :]
                    xp[c, at] = v
                    total = v * v if total is None else total + v * v
                f = factor(total)
                fac[at] = f
                fac_own[at] = f * own[pl.ds(pl.multiple_of(b * per + i, 8), 8)]

    def extended(values, c, m, i):
        down = [values[c, plane(r, i - 1, block)] for r in (m - 2, m - 1)]
        up_ = [values[c, plane(r, i + 1, block)] for r in (0, 1)]
        return down + [values[c, plane(r, i, block)] for r in range(m)] + up_

    def folded(kernel_ref, gain_ref, c):
        return [
            jnp.broadcast_to(kernel_ref[j : j + 1, lanes(c)] * gain_ref[:, lanes(c)], (block, LANES))
            for j in range(5)
        ]

    def taps(c, m, values, factors, gain_ref, kernel_ref, targets):
        k = folded(kernel_ref, gain_ref, c)
        for i in range(0, rows, block):
            f = [factors[plane(r, i - 1, block)] for r in (m - 2, m - 1)]
            f += [factors[plane(r, i, block)] for r in range(m)]
            f += [factors[plane(r, i + 1, block)] for r in (0, 1)]
            ext = [v * w for v, w in zip(extended(values, c, m, i), f)]
            for r in range(m):
                total = k[0] * ext[r]
                for j in range(1, 5):
                    total = total + k[j] * ext[r + j]
                to = slice(r * rows + i, r * rows + i + block)
                targets[0][to, lanes(c)] = total.astype(BF16)
                if len(targets) > 1:
                    if i in edges:
                        total = total * own[i : i + block]
                    targets[1][to, lanes(c)] = total.astype(BF16)

    for load in loads[2:]:
        load.wait()
    pl.loop(0, groups)(lambda c: taps(c, 4, xp, fac, g1_ref, k1_ref, [conv]))

    for k in range(ch // wide):
        for t in range(2):
            part = lanes(k, wide)
            at = slice(2 * t * rows, 2 * (t + 1) * rows)
            pre = jnp.dot(conv[at], w1_ref[:, part], preferred_element_type=F32)
            pre = pre + b1_ref[:, part]
            cdf, density = gelu_parts(pre)
            for q in range(wide // LANES):
                c = k * (wide // LANES) + q
                pooled = None
                for p in range(2):
                    sub = (slice(p * rows, (p + 1) * rows), slice(q * LANES, (q + 1) * LANES))
                    first = (2 * t + p) * rows
                    slope[c, first : first + rows] = cdf[sub] + pre[sub] * density[sub]
                    s = xp[c, plane(2 * t + p)] + pre[sub] * cdf[sub]
                    pooled = s if pooled is None else pooled + s
                up[c, plane(t)] = (pooled * 0.5).astype(BF16).astype(F32)

    for c in range(groups):
        for t in range(2):
            for i in edges:
                up[c, plane(t, i, block)] = up[c, plane(t, i, block)] * inside[i : i + block]
            for p in range(2):
                for i in edges:
                    to = slice((2 * t + p) * rows + i, (2 * t + p) * rows + i + block)
                    conv[to, lanes(c)] = (conv[to, lanes(c)].astype(F32) * own[i : i + block]).astype(BF16)

    for t in range(2):
        for i in range(0, rows, block):
            total = None
            for c in range(groups):
                v = up[c, plane(t, i, block)]
                total = v * v if total is None else total + v * v
            f = factor(total)
            fac2[plane(t, i, block)] = f
            fac2_own[plane(t, i, block)] = f * own[i : i + block] if i in edges else f
    pl.loop(0, groups)(lambda c: taps(c, 2, up, fac2, g2_ref, k2_ref, [conv2, conv2_own]))

    nt = (((1,), (1,)), ((), ()))
    tn = (((0,), (0,)), ((), ()))

    if blocks:
        sums = (rest[0:8], rest[8:16])
        srecv1, ssum, srecv2, sall, sfin, sfrecv, small_send, small_recv = rest[16:24]
        small_sems = (small_send, small_recv)
        widths = (-(-ch2 // 256) * LANES, -(-ch // 256) * LANES)
        starts = (ch2 - widths[0], ch - widths[1])

        def small_part(e, who):
            return pl.ds(pl.multiple_of(who * starts[e], LANES), widths[e])

        def small_copies(e):
            w, k = widths[e], 6 * e
            block = pl.ds(8 * e, 8)
            mine = sall.at[e, z, :, pl.ds(0, w)]
            return (
                [(small_ref.at[block], srecv1.at[e], k, mate)],
                [(ssum.at[e, :, small_part(e, core)], srecv2.at[e, :, pl.ds(0, w)], k + 1, over)],
                [(mine, mine, k + 2 + i, at_z(order[i])) for i in range(3)],
                [(sfin.at[e, :, pl.ds(0, w)], sfrecv.at[e, :, pl.ds(0, w)], k + 5, mate)],
            )

        def small_stage(e, stage):
            copies = small_copies(e)
            w = widths[e]
            if stage:
                for source, target, k, other in copies[stage - 1]:
                    remote(source, target, small_sems, k, other).wait()
            if stage == 1:
                ssum[e] = small_ref[8 * e : 8 * e + 8] + srecv1[e]
            if stage == 2:
                sall[e, z, :, 0:w] = ssum[e, :, small_part(e, core)] + srecv2[e, :, 0:w]
            if stage == 3:
                sfin[e, :, 0:w] = (sall[e, 0, :, 0:w] + sall[e, 1, :, 0:w]) + (
                    sall[e, 2, :, 0:w] + sall[e, 3, :, 0:w]
                )
            if stage == 4:
                small_out[8 * e : 8 * e + 8, small_part(e, core)] = sfin[e, :, 0:w]
                small_out[8 * e : 8 * e + 8, small_part(e, 1 - core)] = sfrecv[e, :, 0:w]
                return
            for source, target, k, other in copies[stage]:
                send(source, target, small_sems, k, other)

        def fill(m, zt, term):
            blk = sums[m][0]
            size = blk.shape[3]
            for d in range(4):
                blk[d % 2, zt, d // 2] = term[d * size : (d + 1) * size].astype(BF16)

        def core_copy(m, zt):
            blk, recv1, sems = sums[m][0], sums[m][1], sums[m][6:8]
            return remote(blk.at[1 - core, zt], recv1.at[zt], sems, zt, mate)

        def y_copy(m, zt):
            send2, recv2, sems = sums[m][2], sums[m][3], sums[m][6:8]
            return remote(send2.at[zt], recv2.at[zt], sems, 4 + zt, over)

        def z_copy(m, zt):
            send3, recv3, sems = sums[m][4], sums[m][5], sums[m][6:8]
            return remote(send3.at[zt], recv3.at[z], sems, (8 + zt, 8 + z), at_z(zt))

        def stage_y(m, zt):
            blk, recv1, send2 = sums[m][:3]
            core_copy(m, zt).wait()
            send2[zt] = (blk[core, zt, 1 - y].astype(F32) + recv1[zt, 1 - y].astype(F32)).astype(BF16)
            y_copy(m, zt).start()

        def half_sum(m, zt):
            blk, recv1, recv2 = sums[m][0], sums[m][1], sums[m][3]
            kept = blk[core, zt, y].astype(F32) + recv1[zt, y].astype(F32)
            return kept + recv2[zt].astype(F32)

        def z_send(m, zt):
            sums[m][4][zt] = half_sum(m, zt).astype(BF16)
            z_copy(m, zt).start()

        def stage_z(m, i):
            zt = order[i] if m == 0 else i
            y_copy(m, zt).wait()
            if m:
                pl.when(z != zt)(lambda: z_send(m, zt))
            elif i < 3:
                z_send(m, zt)

        def stage_end(m, target):
            recv3, sems = sums[m][5], sums[m][6:8]
            total = half_sum(m, z)
            for zt in order[:3]:
                remote(
                    sums[m][4].at[zt], recv3.at[zt], sems, (8 + zt, 8 + zt), at_z(zt)
                ).wait()
                total = total + recv3[zt].astype(F32)
            target[...] = total

    def when_blocks(f, *args):
        if blocks:
            f(*args)

    def own_sum(value):
        total, first = None, 0
        for i in edges + [rows]:
            parts = [value[first:i]] if i > first else []
            if i < rows:
                mask = jnp.concatenate([own[i : i + block]] * (value.shape[1] // LANES), axis=1)
                parts.append(value[i : i + block] * mask)
            for part in parts:
                part = jnp.sum(part, axis=0, keepdims=True)
                total = part if total is None else total + part
            first = i + block
        return total

    quarter = ch2 // 4
    for i, s in enumerate(range(0, ch2, wide)):
        e = min(s + wide, ch2)
        part = slice(s, e)
        pre = jnp.dot(conv2[...], w2_ref[:, part], preferred_element_type=F32) + b2_ref[:, part]
        cdf, density = gelu_parts(pre)
        grad = cot[:, part]
        total = jnp.zeros((1, e - s), F32)
        column = []
        for t in range(2):
            at = slice(t * rows, (t + 1) * rows)
            value = grad * (cdf[at] + pre[at] * density[at])
            column.append(value.astype(BF16))
            back2[at, part] = column[-1]
            total = total + own_sum(value)
        small_ref[6:7, part] = total * scale
        gt[s:e] = (
            lax.dot_general(
                jnp.concatenate(column, axis=0), conv2_own[...], tn, preferred_element_type=F32
            )
            * scale
        )
        if blocks:
            fill(1, i, gt[i * quarter : (i + 1) * quarter])
            core_copy(1, i).start()
            if i >= 2:
                stage_y(1, i - 2)
    if not blocks:
        gt2_ref[...] = gt[0:ch2]

    def kernel_sums(c, m, values, factors, gain_ref, grads, kernel_row):
        totals = [None] * 5
        for i in range(0, rows, block):
            ext = extended(grads, c, m, i)
            for r in range(m):
                at = plane(r, i, block)
                v = values[c, at] * factors[at]
                for j in range(5):
                    term = v * ext[r + 4 - j]
                    totals[j] = term if totals[j] is None else totals[j] + term
        for j in range(5):
            small_ref[kernel_row + j : kernel_row + j + 1, lanes(c)] = (
                jnp.sum(totals[j], axis=0, keepdims=True) * gain_ref[:, lanes(c)]
            ) * scale

    def taps_back(c, m, values, gain_ref, kernel_ref, grads):
        k = folded(kernel_ref, gain_ref, c)
        for i in range(0, rows, block):
            ext = extended(grads, c, m, i)
            for r in range(m):
                at = plane(r, i, block)
                d = k[0] * ext[r + 4]
                for j in range(1, 5):
                    d = d + k[j] * ext[r + 4 - j]
                dn[c, at] = d
                ss[at] += d * values[c, at]

    def inner(m, factors):
        for r in range(m):
            for i in range(0, rows, block):
                at = plane(r, i, block)
                f = factors[at]
                mean = jnp.sum(ss[at], axis=1, keepdims=True) * (1.0 / ch)
                ss[at] = f * f * f * jnp.broadcast_to(mean, f.shape)

    def scatter(target, result, m, k):
        for q in range(wide // LANES):
            for r in range(m):
                target[k * (wide // LANES) + q, plane(r)] = result[
                    r * rows : (r + 1) * rows, q * LANES : (q + 1) * LANES
                ]

    for k in range(ch // wide):
        scatter(
            into2,
            lax.dot_general(back2[...], w2_ref[lanes(k, wide), :], nt, preferred_element_type=F32),
            2,
            k,
        )
        if k < 2:
            when_blocks(lambda: stage_y(1, k + 2))
    ss[...] = jnp.zeros_like(ss)

    @pl.loop(0, groups)
    def _(c):
        kernel_sums(c, 2, up, fac2_own, g2_ref, into2, 0)
        taps_back(c, 2, up, g2_ref, k2_ref, into2)

    inner(2, fac2)

    half = ch // 2
    for h in range(2):
        first = h
        if blocks:
            first = 1 - z // 2 if h == 0 else z // 2

        @pl.loop(0, groups // 2)
        def _(step):
            c = first * (groups // 2) + step
            total = None
            for i in range(0, rows, block):
                for t in range(2):
                    at = plane(t, i, block)
                    grad = cot[i : i + block, lanes(c)]
                    d = (fac2[at] * dn[c, at] - up[c, at] * ss[at] + grad) * 0.5
                    if i in edges:
                        d = d * inside[i : i + block]
                    up[c, at] = d
                    for r in (2 * t, 2 * t + 1):
                        to = slice(r * rows + i, r * rows + i + block)
                        value = d * slope[c, to]
                        back[to, lanes(c)] = value.astype(BF16)
                        if i in edges:
                            value = value * own[i : i + block]
                        total = value if total is None else total + value
            small_ref[5:6, lanes(c)] = jnp.sum(total, axis=0, keepdims=True) * scale

        term = (
            lax.dot_general(
                back[:, lanes(first, half)], conv[...], tn, preferred_element_type=F32
            )
            * scale
        )
        if blocks:
            for i in range(2):
                zt = 2 * first + i
                fill(0, zt, term[i * (half // 2) : (i + 1) * (half // 2)])
                core_copy(0, zt).start()
            stage_z(1, h)
            if h:
                small_stage(0, 0)
        else:
            gt1_ref[h * half : (h + 1) * half] = term

    for k in range(ch // wide):
        scatter(
            into,
            lax.dot_general(back[...], w1_ref[lanes(k, wide), :], nt, preferred_element_type=F32),
            4,
            k,
        )

    if blocks:
        small_stage(0, 1)
        for i in range(3):
            stage_y(0, order[i])
        stage_z(1, 2)
    pl.loop(0, groups)(lambda c: kernel_sums(c, 4, xp, fac_own, g1_ref, into, 8))
    if blocks:
        small_stage(1, 0)
        stage_z(1, 3)
    ss[...] = jnp.zeros_like(ss)

    def first_back(c):
        taps_back(c, 4, xp, g1_ref, k1_ref, into)

    pl.loop(0, groups // 2)(first_back)
    if blocks:
        small_stage(1, 1)
        stage_y(0, order[3])
    pl.loop(groups // 2, groups)(first_back)
    if blocks:
        small_stage(0, 2)
    inner(4, fac)

    def out_copy(c):
        part = lanes(c)
        return pltpu.make_async_copy(fin.at[:, :, part], out_hbm.at[:, :, part], out_sem.at[c])

    def finish(c):
        for i in range(0, rows, block):
            for r in range(4):
                at = plane(r, i, block)
                v = up[c, plane(r // 2, i, block)] + fac[at] * dn[c, at] - xp[c, at] * ss[at]
                mix[pl.ds(4 * i + r, block, stride=4), :] = v
        for b in range(batch):
            base = b * span + HALO
            fin[b, :, lanes(c)] = mix[base : base + length].astype(BF16)
        out_copy(c).start()

    pl.loop(0, groups)(finish)
    if blocks:
        stage_z(0, 0)
        stage_z(0, 1)
        stage_z(0, 2)
        small_stage(1, 2)
        small_stage(0, 3)
        stage_end(1, sum2_ref)
        small_stage(0, 4)
        stage_z(0, 3)
        small_stage(1, 3)
        stage_end(0, sum1_ref)
        small_stage(1, 4)
    else:
        small_out[...] = small_ref[...]
    @pl.loop(0, groups)
    def _(c):
        out_copy(c).wait()


def tail_kernel(fast, p_ref, small_ref, gain1_ref, k1_ref, gain2_ref, k2_ref, *refs):
    count = 3 if fast else 1
    sources = [p_ref] + list(refs[: count - 1])
    targets, refs = refs[count - 1 : 2 * count - 1], refs[2 * count - 1 :]
    b1_out, b2_out, k1_out, k2_out, g1_out, g2_out = refs[:6]
    held, (in_sem, out_sem) = refs[6 : 6 + count], refs[6 + count :]
    moves = []
    for source, middle, target in zip(sources, held, targets):
        parts = [(source, middle, target)]
        if not moves:
            length = p_ref.shape[1]
            step = length // 4
            parts = [
                tuple(ref.at[b, pl.ds(s, step)] for ref in parts[0])
                for b in range(p_ref.shape[0])
                for s in range(0, length, step)
            ]
        for one, two, three in parts:
            k = len(moves)
            moves.append(
                (
                    pltpu.make_async_copy(one, two, in_sem.at[k]),
                    pltpu.make_async_copy(two, three, out_sem.at[k]),
                )
            )
    for move in moves:
        move[0].start()
    ch = b1_out.shape[0]
    b1_out[...] = small_ref[5, :ch]
    b2_out[...] = small_ref[6, :]
    k1_out[...] = small_ref[8:13, :ch]
    k2_out[...] = small_ref[0:5, :ch]
    for row, k_ref, gain_ref, g_out in ((8, k1_ref, gain1_ref, g1_out), (0, k2_ref, gain2_ref, g2_out)):
        total = jnp.sum(small_ref[row : row + 5, :ch] * k_ref[...], axis=0)
        g_out[...] = total / gain_ref[...]
    for move in moves:
        move[0].wait()
        move[1].start()
    for move in moves:
        move[1].wait()


def sums_scratch(ch, ch2, small_shape):
    shapes = []
    for size in (ch // 16, ch2 // 16):
        shapes += [
            pltpu.VMEM((2, 4, 2, size, ch), BF16),
            pltpu.VMEM((4, 2, size, ch), BF16),
            pltpu.VMEM((4, size, ch), BF16),
            pltpu.VMEM((4, size, ch), BF16),
            pltpu.VMEM((4, size, ch), BF16),
            pltpu.VMEM((4, size, ch), BF16),
            pltpu.SemaphoreType.DMA((12,)),
            pltpu.SemaphoreType.DMA((12,)),
        ]
    width = small_shape[1]
    shapes += [pltpu.VMEM((2, 8, width), F32)] * 3 + [pltpu.VMEM((2, 4, 8, width), F32)]
    shapes += [pltpu.VMEM((2, 8, width), F32)] * 2
    return shapes + [pltpu.SemaphoreType.DMA((12,)), pltpu.SemaphoreType.DMA((12,))]


def per_device(fast, n, x, g1, k1, w1, b1, g2, k2, w2, b2, cot):
    batch, length, ch = x.shape
    quarter, ch2 = cot.shape[1:]
    scale = 1.0 / math.sqrt(batch * length * n)
    any_spec = pl.BlockSpec(memory_space=pl.ANY)
    vmem = pl.BlockSpec(memory_space=pltpu.VMEM)

    rows = batch * (length + 2 * HALO) // 4
    small_shape = (16, ch2)
    groups, pitch = ch // LANES, rows + 16
    if fast:
        grads = [jax.ShapeDtypeStruct((k // 16, ch), F32) for k in (ch, ch2)]
    else:
        grads = [jax.ShapeDtypeStruct((ch, ch), F32), jax.ShapeDtypeStruct((ch2, ch), F32)]
    outs = pl.pallas_call(
        functools.partial(step_kernel, scale, n, fast),
        out_shape=[jax.ShapeDtypeStruct(x.shape, BF16)]
        + grads
        + [jax.ShapeDtypeStruct(small_shape, F32)],
        in_specs=[any_spec] + [vmem] * 2 + [any_spec] + [vmem] * 3 + [any_spec, vmem, any_spec],
        out_specs=[any_spec] + [vmem] * (1 + len(grads)),
        scratch_shapes=[
            pltpu.VMEM(x.shape, BF16),
            pltpu.VMEM(cot.shape, BF16),
            pltpu.VMEM((groups, 4 * rows, LANES), F32),
            pltpu.VMEM((groups, 4 * pitch, LANES), F32),
            pltpu.VMEM((4 * pitch, LANES), F32),
            pltpu.VMEM((4 * pitch, LANES), F32),
            pltpu.VMEM((4 * rows, ch), BF16),
            pltpu.VMEM((groups, 4 * rows, LANES), F32),
            pltpu.VMEM((groups, 2 * pitch, LANES), F32),
            pltpu.VMEM((2 * pitch, LANES), F32),
            pltpu.VMEM((2 * pitch, LANES), F32),
            pltpu.VMEM((2 * rows, ch), BF16),
            pltpu.VMEM((2 * rows, ch), BF16),
            pltpu.VMEM((2 * rows, ch2), BF16),
            pltpu.VMEM((groups, 2 * pitch, LANES), F32),
            pltpu.VMEM((rows, ch2), F32),
            pltpu.VMEM((4 * pitch, LANES), F32),
            pltpu.VMEM((rows, LANES), F32),
            pltpu.VMEM((rows, LANES), F32),
            pltpu.VMEM((4 * rows, ch), BF16),
            pltpu.VMEM((groups, 4 * pitch, LANES), F32),
            pltpu.VMEM((groups, 4 * pitch, LANES), F32),
            pltpu.VMEM((ch2, ch), F32),
            pltpu.VMEM((4 * rows, LANES), F32),
            pltpu.VMEM(x.shape, BF16),
            pltpu.VMEM((batch, HALO, ch), BF16),
            pltpu.VMEM((batch, HALO, ch), BF16),
            pltpu.VMEM((batch, HALO, ch2), BF16),
            pltpu.VMEM((batch, HALO, ch2), BF16),
            pltpu.VMEM(w1.shape, BF16),
            pltpu.VMEM(w2.shape, BF16),
            pltpu.VMEM((1, ch), F32),
            pltpu.VMEM((1, ch), F32),
            pltpu.VMEM((1, ch), F32),
            pltpu.VMEM((1, ch2), F32),
            pltpu.VMEM(small_shape, F32),
            pltpu.SemaphoreType.DMA((4,)),
            pltpu.SemaphoreType.DMA((4,)),
            pltpu.SemaphoreType.DMA((4,)),
            pltpu.SemaphoreType.DMA((ch // LANES,)),
        ]
        + (sums_scratch(ch, ch2, small_shape) if fast else []),
        compiler_params=pltpu.CompilerParams(
            collective_id=0, has_side_effects=True, vmem_limit_bytes=60 * 2**20
        ),
        name="step",
    )(x, g1, k1, w1, b1, g2, k2, w2, b2, cot)
    planes, *parts, small = outs
    if not fast:
        grad_w = [
            lax.psum_scatter(part, "seq", scatter_dimension=0, tiled=True).T for part in parts
        ]
        small = lax.psum(small, "seq")
        parts = []

    results = [(ch,), (ch2,), (5, ch), (5, ch), (ch,), (ch,)]
    grad_x, *rest = pl.pallas_call(
        functools.partial(tail_kernel, fast),
        out_shape=[jax.ShapeDtypeStruct(x.shape, BF16)]
        + [jax.ShapeDtypeStruct(part.shape, F32) for part in parts]
        + [jax.ShapeDtypeStruct(shape, F32) for shape in results],
        in_specs=[any_spec] + [vmem] * 5 + [any_spec] * len(parts),
        out_specs=[any_spec] * (1 + len(parts)) + [vmem] * len(results),
        scratch_shapes=[pltpu.VMEM(x.shape, BF16)]
        + [pltpu.VMEM(part.shape, F32) for part in parts]
        + [pltpu.SemaphoreType.DMA((4 * batch + 2,))] * 2,
        name="tail",
    )(planes, small, g1, k1, g2, k2, *parts)
    if fast:
        grad_w, rest = [part.T for part in rest[:2]], rest[2:]
    return (grad_x, *grad_w, *rest)


def solution(mesh):
    n = mesh.shape["seq"]
    return jax.shard_map(
        functools.partial(per_device, n == 16, n),
        mesh=mesh,
        in_specs=(P("groups", "seq", None),) + (P(),) * 8 + (P("groups", "seq", None),),
        out_specs=(
            P("groups", "seq", None),
            P("groups", "seq"),
            P("groups", "seq"),
            P("groups"),
            P("groups"),
            P("groups", None),
            P("groups", None),
            P("groups"),
            P("groups"),
        ),
        check_vma=False,
    )
```

```python
import functools
import math

import jax
import jax.numpy as jnp
from jax import lax
from jax.experimental import pallas as pl
from jax.experimental.pallas import tpu as pltpu
from jax.sharding import PartitionSpec as P

MESH = pl.DeviceIdType.MESH
F32 = jnp.float32
BF16 = jnp.bfloat16
epsilon = 1e-06
inv_sqrt_two = 0.7071067811865476
inv_sqrt_tau = 0.3989422804014327
HALO = 16
LANES = 128


def gelu_parts(v):
    cdf = 0.5 * (1.0 + lax.erf(v * inv_sqrt_two))
    return cdf, jnp.exp(-0.5 * v * v) * inv_sqrt_tau


def step_kernel(
    scale,
    n,
    blocks,
    x_hbm,
    g1_in,
    k1_ref,
    w1_hbm,
    b1_in,
    g2_in,
    k2_ref,
    w2_hbm,
    b2_in,
    c_hbm,
    out_hbm,
    *rest,
):
    if blocks:
        sum1_ref, sum2_ref, small_out = rest[:3]
    else:
        gt1_ref, gt2_ref, small_out = rest[:3]
    (x_ref, c_ref, xs, xp, fac, fac_own, conv, slope, up, fac2, fac2_own, conv2, conv2_own, back2,
     into2, cot, ss, own, inside, back, into, dn, gt, mix, fin, xb_ref, xa_ref, cb_ref, ca_ref,
     w1_ref, w2_ref, g1_ref, b1_ref, g2_ref, b2_ref, small_ref, halo_send, halo_recv, load_sem,
     out_sem) = rest[3:43]
    rest = rest[43:]
    batch, length, ch = x_ref.shape
    ch2 = c_ref.shape[2]
    span = length + 2 * HALO
    per = span // 4
    rows = batch * per
    groups = ch // LANES
    side = HALO // 4
    wide = 256
    pitch = rows + 16
    block = 16
    edges = [i for i in range(0, rows, block) if any((i + j) % per in (0, per - 1) for j in range(block))]

    def plane(r, i=0, size=None):
        first = r * pitch + 8 + i
        return slice(first, first + (rows if size is None else size))

    me = lax.axis_index("seq")
    right, left = lax.rem(me + 1, n), lax.rem(me + n - 1, n)
    others = [left, right]
    if blocks:
        z, y, core = me // 4, lax.rem(me // 2, 2), lax.rem(me, 2)
        mate, over = me + 1 - 2 * core, me + 2 - 4 * y
        near = z + 1 - 2 * lax.rem(z, 2)
        order = [lax.rem(z + 2, 4), lax.rem(near + 2, 4), near, z]

        def at_z(zt):
            return zt * 4 + y * 2 + core

        others += [mate, over] + [at_z(zt) for zt in order[:3]]
    loads = [
        pltpu.make_async_copy(source, target, load_sem.at[k])
        for k, (source, target) in enumerate(
            ((x_hbm, x_ref), (c_hbm, c_ref), (w1_hbm, w1_ref), (w2_hbm, w2_ref))
        )
    ]
    barrier = pltpu.get_barrier_semaphore()
    for other in others:
        pl.semaphore_signal(barrier, inc=1, device_id={"seq": other}, device_id_type=MESH)
    for load in loads:
        load.start()
    for source, target in ((g1_in, g1_ref), (b1_in, b1_ref), (g2_in, g2_ref), (b2_in, b2_ref)):
        target[...] = source[...].reshape(target.shape)

    within = lax.broadcasted_iota(jnp.int32, (rows, LANES), 0)
    for b in range(1, batch):
        within = jnp.where(within >= per, within - per, within)
    is_own = (within >= side) & (within < per - side)
    own[...] = jnp.where(is_own, 1.0, 0.0)
    at_first, at_last = me == 0, me == n - 1
    low = jnp.where(at_first, side, 0)
    high = jnp.where(at_last, per - side, per)
    inside[...] = jnp.where((within >= low) & (within < high), 1.0, 0.0)
    small_ref[...] = jnp.zeros_like(small_ref)
    for ref, m in ((fac, 4), (fac_own, 4), (fac2, 2), (fac2_own, 2)):
        for r in range(m):
            for i in (-8, rows):
                ref[plane(r, i, 8)] = jnp.zeros((8, LANES), F32)
    for ref, m in ((xp, 4), (into, 4), (up, 2), (into2, 2)):
        for r in range(m):
            for i in (-8, rows):
                ref[:, plane(r, i, 8)] = jnp.zeros((groups, 8, LANES), F32)
    pl.semaphore_wait(barrier, len(others))

    def remote(source, target, sems, k, other):
        if not isinstance(k, tuple):
            k = (k, k)
        return pltpu.make_async_remote_copy(
            src_ref=source,
            dst_ref=target,
            send_sem=sems[0].at[k[0]],
            recv_sem=sems[1].at[k[1]],
            device_id={"seq": other},
            device_id_type=MESH,
        )

    def send(*args):
        copy = remote(*args)
        copy.start()
        return copy

    halo = []
    for ref, before, after in ((x_hbm, xb_ref, xa_ref), (c_hbm, cb_ref, ca_ref)):
        last = ref.shape[1] - HALO
        for source, target, other in (
            (ref.at[:, pl.ds(last, HALO)], before, right),
            (ref.at[:, pl.ds(0, HALO)], after, left),
        ):
            halo.append(send(source, target, (halo_send, halo_recv), len(halo), other))

    def lanes(c, width=LANES):
        if isinstance(c, int):
            return slice(c * width, (c + 1) * width)
        return pl.ds(pl.multiple_of(c * width, width), width)

    loads[0].wait()

    @pl.loop(0, groups)
    def _(c):
        for b in range(batch):
            base = b * span + HALO
            xs[c, base : base + length] = x_ref[b, :, lanes(c)].astype(F32)

    def factor(total):
        return jnp.broadcast_to(
            lax.rsqrt(jnp.sum(total, axis=1, keepdims=True) * (1.0 / ch) + epsilon), total.shape
        )

    def load_planes(starts):
        @pl.loop(0, batch)
        def _(b):
            for i in starts:
                for r in range(4):
                    at = pl.ds(pl.multiple_of(b * per + (r * pitch + 8 + i), 8), 8)
                    total = None
                    for c in range(groups):
                        v = xs[c, pl.ds(b * span + (4 * i + r), 8, stride=4), :]
                        xp[c, at] = v
                        total = v * v if total is None else total + v * v
                    f = factor(total)
                    fac[at] = f
                    fac_own[at] = f * own[pl.ds(pl.multiple_of(b * per + i, 8), 8)]

    def extended(values, c, m, i):
        down = [values[c, plane(r, i - 1, block)] for r in (m - 2, m - 1)]
        up_ = [values[c, plane(r, i + 1, block)] for r in (0, 1)]
        return down + [values[c, plane(r, i, block)] for r in range(m)] + up_

    def folded(kernel_ref, gain_ref, c):
        return [
            jnp.broadcast_to(kernel_ref[j : j + 1, lanes(c)] * gain_ref[:, lanes(c)], (block, LANES))
            for j in range(5)
        ]

    def taps(c, m, values, factors, gain_ref, kernel_ref, targets, starts):
        k = folded(kernel_ref, gain_ref, c)
        for i in starts:
            f = [factors[plane(r, i - 1, block)] for r in (m - 2, m - 1)]
            f += [factors[plane(r, i, block)] for r in range(m)]
            f += [factors[plane(r, i + 1, block)] for r in (0, 1)]
            ext = [v * w for v, w in zip(extended(values, c, m, i), f)]
            for r in range(m):
                total = k[0] * ext[r]
                for j in range(1, 5):
                    total = total + k[j] * ext[r + j]
                to = slice(r * rows + i, r * rows + i + block)
                targets[0][to, lanes(c)] = total.astype(BF16)
                if len(targets) > 1:
                    if i in edges:
                        total = total * own[i : i + block]
                    targets[1][to, lanes(c)] = total.astype(BF16)

    outer = [b * per + i for b in range(batch) for i in (0, per - 8)]
    inner_blocks = [
        i
        for i in range(block, rows - block, block)
        if not any(i - 1 < j + 8 and i + block >= j for j in outer)
    ]
    outer_blocks = [i for i in range(0, rows, block) if i not in inner_blocks]

    def project_first(starts):
        ranges = []
        for i in starts:
            if ranges and ranges[-1][1] == i:
                ranges[-1][1] = i + block
            else:
                ranges.append([i, i + block])
        size = len(starts) * block
        for k in range(ch // wide):
            for t in range(2):
                part = lanes(k, wide)
                first = [(2 * t + p) * rows for p in range(2)]
                matrix = jnp.concatenate([conv[f + i : f + e] for f in first for i, e in ranges], axis=0)
                pre = jnp.dot(matrix, w1_ref[:, part], preferred_element_type=F32)
                pre = pre + b1_ref[:, part]
                cdf, density = gelu_parts(pre)
                for q in range(wide // LANES):
                    c = k * (wide // LANES) + q
                    offset = 0
                    for i, e in ranges:
                        pooled = None
                        for p in range(2):
                            start = p * size + offset
                            sub = (slice(start, start + e - i), slice(q * LANES, (q + 1) * LANES))
                            slope[c, first[p] + i : first[p] + e] = cdf[sub] + pre[sub] * density[sub]
                            v = xp[c, plane(2 * t + p, i, e - i)] + pre[sub] * cdf[sub]
                            pooled = v if pooled is None else pooled + v
                        up[c, plane(t, i, e - i)] = (pooled * 0.5).astype(BF16).astype(F32)
                        offset += e - i

    def first_section(starts):
        pl.loop(0, groups)(lambda c: taps(c, 4, xp, fac, g1_ref, k1_ref, [conv], starts))
        project_first(starts)

    load_planes(range(8, per - 8, 8))
    loads[2].wait()
    first_section(inner_blocks)

    loads[1].wait()
    for b in range(batch):
        cot[b * per + side : (b + 1) * per - side] = c_ref[b].astype(F32) * 0.5
    for copy in halo:
        copy.wait()

    for b in range(batch):
        base = b * per
        first = cb_ref[b].astype(F32)[HALO - side :] * 0.5
        last = ca_ref[b].astype(F32)[:side] * 0.5
        cot[base : base + side] = jnp.where(at_first, 0.0, first)
        cot[base + per - side : base + per] = jnp.where(at_last, 0.0, last)

    for c in range(groups):
        for b in range(batch):
            base = b * span
            xs[c, base : base + HALO] = jnp.where(at_first, 0.0, xb_ref[b, :, lanes(c)].astype(F32))
            xs[c, base + HALO + length : base + span] = jnp.where(
                at_last, 0.0, xa_ref[b, :, lanes(c)].astype(F32)
            )

    load_planes((0, per - 8))
    first_section(outer_blocks)
    loads[3].wait()

    for c in range(groups):
        for t in range(2):
            for i in edges:
                up[c, plane(t, i, block)] = up[c, plane(t, i, block)] * inside[i : i + block]
            for p in range(2):
                for i in edges:
                    to = slice((2 * t + p) * rows + i, (2 * t + p) * rows + i + block)
                    conv[to, lanes(c)] = (conv[to, lanes(c)].astype(F32) * own[i : i + block]).astype(BF16)

    for t in range(2):
        for i in range(0, rows, block):
            total = None
            for c in range(groups):
                v = up[c, plane(t, i, block)]
                total = v * v if total is None else total + v * v
            f = factor(total)
            fac2[plane(t, i, block)] = f
            fac2_own[plane(t, i, block)] = f * own[i : i + block] if i in edges else f
    pl.loop(0, groups)(lambda c: taps(c, 2, up, fac2, g2_ref, k2_ref, [conv2, conv2_own], range(0, rows, block)))

    nt = (((1,), (1,)), ((), ()))
    tn = (((0,), (0,)), ((), ()))

    if blocks:
        sums = (rest[0:8], rest[8:16])
        srecv1, ssum, srecv2, sall, sfin, sfrecv, small_send, small_recv = rest[16:24]
        small_sems = (small_send, small_recv)
        widths = (-(-ch2 // 256) * LANES, -(-ch // 256) * LANES)
        starts = (ch2 - widths[0], ch - widths[1])

        def small_part(e, who):
            return pl.ds(pl.multiple_of(who * starts[e], LANES), widths[e])

        def small_copies(e):
            w, k = widths[e], 6 * e
            block = pl.ds(8 * e, 8)
            mine = sall.at[e, z, :, pl.ds(0, w)]
            return (
                [(small_ref.at[block], srecv1.at[e], k, mate)],
                [(ssum.at[e, :, small_part(e, core)], srecv2.at[e, :, pl.ds(0, w)], k + 1, over)],
                [(mine, mine, k + 2 + i, at_z(order[i])) for i in range(3)],
                [(sfin.at[e, :, pl.ds(0, w)], sfrecv.at[e, :, pl.ds(0, w)], k + 5, mate)],
            )

        def small_stage(e, stage):
            copies = small_copies(e)
            w = widths[e]
            if stage:
                for source, target, k, other in copies[stage - 1]:
                    remote(source, target, small_sems, k, other).wait()
            if stage == 1:
                ssum[e] = small_ref[8 * e : 8 * e + 8] + srecv1[e]
            if stage == 2:
                sall[e, z, :, 0:w] = ssum[e, :, small_part(e, core)] + srecv2[e, :, 0:w]
            if stage == 3:
                sfin[e, :, 0:w] = (sall[e, 0, :, 0:w] + sall[e, 1, :, 0:w]) + (
                    sall[e, 2, :, 0:w] + sall[e, 3, :, 0:w]
                )
            if stage == 4:
                small_out[8 * e : 8 * e + 8, small_part(e, core)] = sfin[e, :, 0:w]
                small_out[8 * e : 8 * e + 8, small_part(e, 1 - core)] = sfrecv[e, :, 0:w]
                return
            for source, target, k, other in copies[stage]:
                send(source, target, small_sems, k, other)

        def fill(m, zt, term):
            blk = sums[m][0]
            size = blk.shape[3]
            for d in range(4):
                blk[d % 2, zt, d // 2] = term[d * size : (d + 1) * size].astype(BF16)

        def core_copy(m, zt):
            blk, recv1, sems = sums[m][0], sums[m][1], sums[m][6:8]
            return remote(blk.at[1 - core, zt], recv1.at[zt], sems, zt, mate)

        def y_copy(m, zt):
            send2, recv2, sems = sums[m][2], sums[m][3], sums[m][6:8]
            return remote(send2.at[zt], recv2.at[zt], sems, 4 + zt, over)

        def z_copy(m, zt):
            send3, recv3, sems = sums[m][4], sums[m][5], sums[m][6:8]
            return remote(send3.at[zt], recv3.at[z], sems, (8 + zt, 8 + z), at_z(zt))

        def stage_y(m, zt):
            blk, recv1, send2 = sums[m][:3]
            core_copy(m, zt).wait()
            send2[zt] = (blk[core, zt, 1 - y].astype(F32) + recv1[zt, 1 - y].astype(F32)).astype(BF16)
            y_copy(m, zt).start()

        def half_sum(m, zt):
            blk, recv1, recv2 = sums[m][0], sums[m][1], sums[m][3]
            kept = blk[core, zt, y].astype(F32) + recv1[zt, y].astype(F32)
            return kept + recv2[zt].astype(F32)

        def z_send(m, zt):
            sums[m][4][zt] = half_sum(m, zt).astype(BF16)
            z_copy(m, zt).start()

        def stage_z(m, i):
            zt = order[i]
            y_copy(m, zt).wait()
            if i < 3:
                z_send(m, zt)

        def stage_end(m, target):
            recv3, sems = sums[m][5], sums[m][6:8]
            total = half_sum(m, z)
            for zt in order[:3]:
                remote(
                    sums[m][4].at[zt], recv3.at[zt], sems, (8 + zt, 8 + zt), at_z(zt)
                ).wait()
                total = total + recv3[zt].astype(F32)
            target[...] = total

    def own_sum(value):
        total, first = None, 0
        for i in edges + [rows]:
            parts = [value[first:i]] if i > first else []
            if i < rows:
                mask = jnp.concatenate([own[i : i + block]] * (value.shape[1] // LANES), axis=1)
                parts.append(value[i : i + block] * mask)
            for part in parts:
                part = jnp.sum(part, axis=0, keepdims=True)
                total = part if total is None else total + part
            first = i + block
        return total

    quarter = ch2 // 4
    for s in range(0, ch2, wide):
        e = min(s + wide, ch2)
        part = slice(s, e)
        pre = jnp.dot(conv2[...], w2_ref[:, part], preferred_element_type=F32) + b2_ref[:, part]
        cdf, density = gelu_parts(pre)
        grad = cot[:, part]
        total = jnp.zeros((1, e - s), F32)
        for t in range(2):
            at = slice(t * rows, (t + 1) * rows)
            value = grad * (cdf[at] + pre[at] * density[at])
            back2[at, part] = value.astype(BF16)
            total = total + own_sum(value)
        small_ref[6:7, part] = total * scale

    if blocks:
        halves = (1 - z // 2, z // 2)
        over_half = -(-ch2 // 256) * LANES
        skip = ch2 // 2 - (ch2 - over_half)
        for first in halves:
            columns = pl.ds(pl.multiple_of(first * (ch2 - over_half), LANES), over_half)
            gt[0:over_half] = (
                lax.dot_general(
                    back2[:, columns], conv2_own[...], tn, preferred_element_type=F32
                )
                * scale
            )
            for i in range(2):
                zt = 2 * first + i
                start = pl.multiple_of(first * skip + i * quarter, 8)
                fill(1, zt, gt[pl.ds(start, quarter)])
                core_copy(1, zt).start()
    else:
        gt2_ref[...] = (
            lax.dot_general(back2[...], conv2_own[...], tn, preferred_element_type=F32) * scale
        )

    def taps_back(c, m, values, factors, gain_ref, kernel_ref, grads, kernel_row):
        k = folded(kernel_ref, gain_ref, c)
        totals = [None] * 5
        for i in range(0, rows, block):
            ext = extended(grads, c, m, i)
            for r in range(m):
                at = plane(r, i, block)
                v = values[c, at]
                vf = v * factors[at]
                for j in range(5):
                    term = vf * ext[r + 4 - j]
                    totals[j] = term if totals[j] is None else totals[j] + term
                d = k[0] * ext[r + 4]
                for j in range(1, 5):
                    d = d + k[j] * ext[r + 4 - j]
                dn[c, at] = d
                ss[at] += d * v
        for j in range(5):
            small_ref[kernel_row + j : kernel_row + j + 1, lanes(c)] = (
                jnp.sum(totals[j], axis=0, keepdims=True) * gain_ref[:, lanes(c)]
            ) * scale

    def inner(m, factors):
        for r in range(m):
            for i in range(0, rows, block):
                at = plane(r, i, block)
                f = factors[at]
                mean = jnp.sum(ss[at], axis=1, keepdims=True) * (1.0 / ch)
                ss[at] = f * f * f * jnp.broadcast_to(mean, f.shape)

    def scatter(target, result, m, k):
        for q in range(wide // LANES):
            for r in range(m):
                target[k * (wide // LANES) + q, plane(r)] = result[
                    r * rows : (r + 1) * rows, q * LANES : (q + 1) * LANES
                ]

    for k in range(ch // wide):
        scatter(
            into2,
            lax.dot_general(back2[...], w2_ref[lanes(k, wide), :], nt, preferred_element_type=F32),
            2,
            k,
        )
        if blocks and k == 0:
            stage_y(1, order[0])
            stage_y(1, order[1])
        if blocks and k == 1:
            stage_y(1, order[2])
    ss[...] = jnp.zeros_like(ss)

    @pl.loop(0, groups)
    def _(c):
        taps_back(c, 2, up, fac2_own, g2_ref, k2_ref, into2, 0)

    if blocks:
        small_stage(0, 0)
    inner(2, fac2)

    half = ch // 2
    for h in range(2):
        first = halves[h] if blocks else h

        @pl.loop(0, groups // 2)
        def _(step):
            c = first * (groups // 2) + step
            total = None
            for i in range(0, rows, block):
                for t in range(2):
                    at = plane(t, i, block)
                    grad = cot[i : i + block, lanes(c)]
                    d = (fac2[at] * dn[c, at] - up[c, at] * ss[at] + grad) * 0.5
                    if i in edges:
                        d = d * inside[i : i + block]
                    up[c, at] = d
                    for r in (2 * t, 2 * t + 1):
                        to = slice(r * rows + i, r * rows + i + block)
                        value = d * slope[c, to]
                        back[to, lanes(c)] = value.astype(BF16)
                        if i in edges:
                            value = value * own[i : i + block]
                        total = value if total is None else total + value
            small_ref[13:14, lanes(c)] = jnp.sum(total, axis=0, keepdims=True) * scale

        term = (
            lax.dot_general(
                back[:, lanes(first, half)], conv[...], tn, preferred_element_type=F32
            )
            * scale
        )
        if blocks:
            for i in range(2):
                zt = 2 * first + i
                fill(0, zt, term[i * (half // 2) : (i + 1) * (half // 2)])
                core_copy(0, zt).start()
            if h:
                stage_y(0, order[0])
                stage_y(0, order[1])
            else:
                small_stage(0, 1)
                stage_y(1, order[3])
            stage_z(1, h)
        else:
            gt1_ref[h * half : (h + 1) * half] = term

    for k in range(ch // wide):
        scatter(
            into,
            lax.dot_general(back[...], w1_ref[lanes(k, wide), :], nt, preferred_element_type=F32),
            4,
            k,
        )

    if blocks:
        stage_y(0, order[2])
        stage_z(1, 2)
    ss[...] = jnp.zeros_like(ss)

    def first_back(c):
        taps_back(c, 4, xp, fac_own, g1_ref, k1_ref, into, 8)

    pl.loop(0, groups // 2)(first_back)
    if blocks:
        stage_z(1, 3)
    pl.loop(groups // 2, groups)(first_back)
    if blocks:
        small_stage(1, 0)
        small_stage(0, 2)
        stage_z(0, 0)
    inner(4, fac)

    def out_copy(c):
        part = lanes(c)
        return pltpu.make_async_copy(fin.at[:, :, part], out_hbm.at[:, :, part], out_sem.at[c])

    def finish(c):
        for i in range(0, rows, block):
            for r in range(4):
                at = plane(r, i, block)
                v = up[c, plane(r // 2, i, block)] + fac[at] * dn[c, at] - xp[c, at] * ss[at]
                mix[pl.ds(4 * i + r, block, stride=4), :] = v
        for b in range(batch):
            base = b * span + HALO
            fin[b, :, lanes(c)] = mix[base : base + length].astype(BF16)
        out_copy(c).start()

    pl.loop(0, groups // 2)(finish)
    if blocks:
        small_stage(1, 1)
        stage_y(0, order[3])
        stage_z(0, 1)
    pl.loop(groups // 2, groups)(finish)
    if blocks:
        stage_z(0, 2)
        small_stage(1, 2)
        small_stage(0, 3)
        stage_end(1, sum2_ref)
        stage_z(0, 3)
        small_stage(0, 4)
        small_stage(1, 3)
        stage_end(0, sum1_ref)
        small_stage(1, 4)
    else:
        small_out[...] = small_ref[...]
    @pl.loop(0, groups)
    def _(c):
        out_copy(c).wait()


def tail_kernel(fast, p_ref, small_ref, gain1_ref, k1_ref, gain2_ref, k2_ref, *refs):
    count = 3 if fast else 1
    sources = [p_ref] + list(refs[: count - 1])
    targets, refs = refs[count - 1 : 2 * count - 1], refs[2 * count - 1 :]
    b1_out, b2_out, k1_out, k2_out, g1_out, g2_out = refs[:6]
    held, (in_sem, out_sem) = refs[6 : 6 + count], refs[6 + count :]
    moves = []
    for source, middle, target in zip(sources, held, targets):
        parts = [(source, middle, target)]
        if not moves:
            length = p_ref.shape[1]
            step = length // 4
            parts = [
                tuple(ref.at[b, pl.ds(s, step)] for ref in parts[0])
                for b in range(p_ref.shape[0])
                for s in range(0, length, step)
            ]
        for one, two, three in parts:
            k = len(moves)
            moves.append(
                (
                    pltpu.make_async_copy(one, two, in_sem.at[k]),
                    pltpu.make_async_copy(two, three, out_sem.at[k]),
                )
            )
    for move in moves:
        move[0].start()
    ch = b1_out.shape[0]
    b1_out[...] = small_ref[13, :ch]
    b2_out[...] = small_ref[6, :]
    k1_out[...] = small_ref[8:13, :ch]
    k2_out[...] = small_ref[0:5, :ch]
    for row, k_ref, gain_ref, g_out in ((8, k1_ref, gain1_ref, g1_out), (0, k2_ref, gain2_ref, g2_out)):
        total = jnp.sum(small_ref[row : row + 5, :ch] * k_ref[...], axis=0)
        g_out[...] = total / gain_ref[...]
    for move in moves:
        move[0].wait()
        move[1].start()
    for move in moves:
        move[1].wait()


def sums_scratch(ch, ch2, small_shape):
    shapes = []
    for size in (ch // 16, ch2 // 16):
        shapes += [
            pltpu.VMEM((2, 4, 2, size, ch), BF16),
            pltpu.VMEM((4, 2, size, ch), BF16),
            pltpu.VMEM((4, size, ch), BF16),
            pltpu.VMEM((4, size, ch), BF16),
            pltpu.VMEM((4, size, ch), BF16),
            pltpu.VMEM((4, size, ch), BF16),
            pltpu.SemaphoreType.DMA((12,)),
            pltpu.SemaphoreType.DMA((12,)),
        ]
    width = small_shape[1]
    shapes += [pltpu.VMEM((2, 8, width), F32)] * 3 + [pltpu.VMEM((2, 4, 8, width), F32)]
    shapes += [pltpu.VMEM((2, 8, width), F32)] * 2
    return shapes + [pltpu.SemaphoreType.DMA((12,)), pltpu.SemaphoreType.DMA((12,))]


def per_device(fast, n, x, g1, k1, w1, b1, g2, k2, w2, b2, cot):
    batch, length, ch = x.shape
    quarter, ch2 = cot.shape[1:]
    scale = 1.0 / math.sqrt(batch * length * n)
    any_spec = pl.BlockSpec(memory_space=pl.ANY)
    vmem = pl.BlockSpec(memory_space=pltpu.VMEM)

    rows = batch * (length + 2 * HALO) // 4
    small_shape = (16, ch2)
    groups, pitch = ch // LANES, rows + 16
    if fast:
        grads = [jax.ShapeDtypeStruct((k // 16, ch), F32) for k in (ch, ch2)]
    else:
        grads = [jax.ShapeDtypeStruct((ch, ch), F32), jax.ShapeDtypeStruct((ch2, ch), F32)]
    outs = pl.pallas_call(
        functools.partial(step_kernel, scale, n, fast),
        out_shape=[jax.ShapeDtypeStruct(x.shape, BF16)]
        + grads
        + [jax.ShapeDtypeStruct(small_shape, F32)],
        in_specs=[any_spec] + [vmem] * 2 + [any_spec] + [vmem] * 3 + [any_spec, vmem, any_spec],
        out_specs=[any_spec] + [vmem] * (1 + len(grads)),
        scratch_shapes=[
            pltpu.VMEM(x.shape, BF16),
            pltpu.VMEM(cot.shape, BF16),
            pltpu.VMEM((groups, 4 * rows, LANES), F32),
            pltpu.VMEM((groups, 4 * pitch, LANES), F32),
            pltpu.VMEM((4 * pitch, LANES), F32),
            pltpu.VMEM((4 * pitch, LANES), F32),
            pltpu.VMEM((4 * rows, ch), BF16),
            pltpu.VMEM((groups, 4 * rows, LANES), F32),
            pltpu.VMEM((groups, 2 * pitch, LANES), F32),
            pltpu.VMEM((2 * pitch, LANES), F32),
            pltpu.VMEM((2 * pitch, LANES), F32),
            pltpu.VMEM((2 * rows, ch), BF16),
            pltpu.VMEM((2 * rows, ch), BF16),
            pltpu.VMEM((2 * rows, ch2), BF16),
            pltpu.VMEM((groups, 2 * pitch, LANES), F32),
            pltpu.VMEM((rows, ch2), F32),
            pltpu.VMEM((4 * pitch, LANES), F32),
            pltpu.VMEM((rows, LANES), F32),
            pltpu.VMEM((rows, LANES), F32),
            pltpu.VMEM((4 * rows, ch), BF16),
            pltpu.VMEM((groups, 4 * pitch, LANES), F32),
            pltpu.VMEM((groups, 4 * pitch, LANES), F32),
            pltpu.VMEM((ch2, ch), F32),
            pltpu.VMEM((4 * rows, LANES), F32),
            pltpu.VMEM(x.shape, BF16),
            pltpu.VMEM((batch, HALO, ch), BF16),
            pltpu.VMEM((batch, HALO, ch), BF16),
            pltpu.VMEM((batch, HALO, ch2), BF16),
            pltpu.VMEM((batch, HALO, ch2), BF16),
            pltpu.VMEM(w1.shape, BF16),
            pltpu.VMEM(w2.shape, BF16),
            pltpu.VMEM((1, ch), F32),
            pltpu.VMEM((1, ch), F32),
            pltpu.VMEM((1, ch), F32),
            pltpu.VMEM((1, ch2), F32),
            pltpu.VMEM(small_shape, F32),
            pltpu.SemaphoreType.DMA((4,)),
            pltpu.SemaphoreType.DMA((4,)),
            pltpu.SemaphoreType.DMA((4,)),
            pltpu.SemaphoreType.DMA((ch // LANES,)),
        ]
        + (sums_scratch(ch, ch2, small_shape) if fast else []),
        compiler_params=pltpu.CompilerParams(
            collective_id=0, has_side_effects=True, vmem_limit_bytes=60 * 2**20
        ),
        name="step",
    )(x, g1, k1, w1, b1, g2, k2, w2, b2, cot)
    planes, *parts, small = outs
    if not fast:
        grad_w = [
            lax.psum_scatter(part, "seq", scatter_dimension=0, tiled=True).T for part in parts
        ]
        small = lax.psum(small, "seq")
        parts = []

    results = [(ch,), (ch2,), (5, ch), (5, ch), (ch,), (ch,)]
    grad_x, *rest = pl.pallas_call(
        functools.partial(tail_kernel, fast),
        out_shape=[jax.ShapeDtypeStruct(x.shape, BF16)]
        + [jax.ShapeDtypeStruct(part.shape, F32) for part in parts]
        + [jax.ShapeDtypeStruct(shape, F32) for shape in results],
        in_specs=[any_spec] + [vmem] * 5 + [any_spec] * len(parts),
        out_specs=[any_spec] * (1 + len(parts)) + [vmem] * len(results),
        scratch_shapes=[pltpu.VMEM(x.shape, BF16)]
        + [pltpu.VMEM(part.shape, F32) for part in parts]
        + [pltpu.SemaphoreType.DMA((4 * batch + 2,))] * 2,
        name="tail",
    )(planes, small, g1, k1, g2, k2, *parts)
    if fast:
        grad_w, rest = [part.T for part in rest[:2]], rest[2:]
    return (grad_x, *grad_w, *rest)


def solution(mesh):
    n = mesh.shape["seq"]
    return jax.shard_map(
        functools.partial(per_device, n == 16, n),
        mesh=mesh,
        in_specs=(P("groups", "seq", None),) + (P(),) * 8 + (P("groups", "seq", None),),
        out_specs=(
            P("groups", "seq", None),
            P("groups", "seq"),
            P("groups", "seq"),
            P("groups"),
            P("groups"),
            P("groups", None),
            P("groups", None),
            P("groups"),
            P("groups"),
        ),
        check_vma=False,
    )
```

```python
import functools
import math

import jax
import jax.numpy as jnp
from jax import lax
from jax.experimental import pallas as pl
from jax.experimental.pallas import tpu as pltpu
from jax.sharding import PartitionSpec as P

MESH = pl.DeviceIdType.MESH
F32 = jnp.float32
BF16 = jnp.bfloat16
epsilon = 1e-06
inv_sqrt_two = 0.7071067811865476
inv_sqrt_tau = 0.3989422804014327
HALO = 16
LANES = 128


def gelu_parts(v):
    cdf = 0.5 * (1.0 + lax.erf(v * inv_sqrt_two))
    return cdf, jnp.exp(-0.5 * v * v) * inv_sqrt_tau


def step_kernel(
    scale,
    n,
    blocks,
    x_hbm,
    g1_in,
    k1_ref,
    w1_hbm,
    b1_in,
    g2_in,
    k2_ref,
    w2_hbm,
    b2_in,
    c_hbm,
    out_hbm,
    *rest,
):
    if blocks:
        sum1_ref, sum2_ref, small_out = rest[:3]
    else:
        gt1_ref, gt2_ref, small_out = rest[:3]
    (x_ref, c_ref, xs, xp, fac, fac_own, conv, slope, up, fac2, fac2_own, conv2, conv2_own, back2,
     into2, cot, ss, own, inside, back, into, dn, gt, mix, fin, xb_ref, xa_ref, cb_ref, ca_ref,
     w1_ref, w2_ref, g1_ref, b1_ref, g2_ref, b2_ref, small_ref, halo_send, halo_recv, load_sem,
     out_sem) = rest[3:43]
    rest = rest[43:]
    batch, length, ch = x_ref.shape
    ch2 = c_ref.shape[2]
    span = length + 2 * HALO
    per = span // 4
    rows = batch * per
    groups = ch // LANES
    side = HALO // 4
    wide = 256
    pitch = rows + 16
    block = 16
    edges = [i for i in range(0, rows, block) if any((i + j) % per in (0, per - 1) for j in range(block))]

    def plane(r, i=0, size=None):
        first = r * pitch + 8 + i
        return slice(first, first + (rows if size is None else size))

    me = lax.axis_index("seq")
    right, left = lax.rem(me + 1, n), lax.rem(me + n - 1, n)
    others = [left, right]
    if blocks:
        z, y, core = me // 4, lax.rem(me // 2, 2), lax.rem(me, 2)
        mate, over = me + 1 - 2 * core, me + 2 - 4 * y
        near = z + 1 - 2 * lax.rem(z, 2)
        order = [lax.rem(z + 2, 4), lax.rem(near + 2, 4), near, z]

        def at_z(zt):
            return zt * 4 + y * 2 + core

        others += [mate, over] + [at_z(zt) for zt in order[:3]]
    loads = [
        pltpu.make_async_copy(source, target, load_sem.at[k])
        for k, (source, target) in enumerate(
            ((x_hbm, x_ref), (c_hbm, c_ref), (w1_hbm, w1_ref), (w2_hbm, w2_ref))
        )
    ]
    barrier = pltpu.get_barrier_semaphore()
    for other in others:
        pl.semaphore_signal(barrier, inc=1, device_id={"seq": other}, device_id_type=MESH)
    for load in loads:
        load.start()
    for source, target in ((g1_in, g1_ref), (b1_in, b1_ref), (g2_in, g2_ref), (b2_in, b2_ref)):
        target[...] = source[...].reshape(target.shape)

    within = lax.broadcasted_iota(jnp.int32, (rows, LANES), 0)
    for b in range(1, batch):
        within = jnp.where(within >= per, within - per, within)
    is_own = (within >= side) & (within < per - side)
    own[...] = jnp.where(is_own, 1.0, 0.0)
    at_first, at_last = me == 0, me == n - 1
    low = jnp.where(at_first, side, 0)
    high = jnp.where(at_last, per - side, per)
    inside[...] = jnp.where((within >= low) & (within < high), 1.0, 0.0)
    small_ref[...] = jnp.zeros_like(small_ref)
    for ref, m in ((fac, 4), (fac_own, 4), (fac2, 2), (fac2_own, 2)):
        for r in range(m):
            for i in (-8, rows):
                ref[plane(r, i, 8)] = jnp.zeros((8, LANES), F32)
    for ref, m in ((xp, 4), (into, 4), (up, 2), (into2, 2)):
        for r in range(m):
            for i in (-8, rows):
                ref[:, plane(r, i, 8)] = jnp.zeros((groups, 8, LANES), F32)
    pl.semaphore_wait(barrier, len(others))

    def remote(source, target, sems, k, other):
        if not isinstance(k, tuple):
            k = (k, k)
        return pltpu.make_async_remote_copy(
            src_ref=source,
            dst_ref=target,
            send_sem=sems[0].at[k[0]],
            recv_sem=sems[1].at[k[1]],
            device_id={"seq": other},
            device_id_type=MESH,
        )

    def send(*args):
        copy = remote(*args)
        copy.start()
        return copy

    halo = []
    for ref, before, after in ((x_hbm, xb_ref, xa_ref), (c_hbm, cb_ref, ca_ref)):
        last = ref.shape[1] - HALO
        for source, target, other in (
            (ref.at[:, pl.ds(last, HALO)], before, right),
            (ref.at[:, pl.ds(0, HALO)], after, left),
        ):
            halo.append(send(source, target, (halo_send, halo_recv), len(halo), other))

    def lanes(c, width=LANES):
        if isinstance(c, int):
            return slice(c * width, (c + 1) * width)
        return pl.ds(pl.multiple_of(c * width, width), width)

    loads[0].wait()

    @pl.loop(0, groups)
    def _(c):
        for b in range(batch):
            base = b * span + HALO
            xs[c, base : base + length] = x_ref[b, :, lanes(c)].astype(F32)

    def factor(total):
        return jnp.broadcast_to(
            lax.rsqrt(jnp.sum(total, axis=1, keepdims=True) * (1.0 / ch) + epsilon), total.shape
        )

    def load_planes(starts):
        @pl.loop(0, batch)
        def _(b):
            for i in starts:
                for r in range(4):
                    at = pl.ds(pl.multiple_of(b * per + (r * pitch + 8 + i), 8), 8)
                    total = None
                    for c in range(groups):
                        v = xs[c, pl.ds(b * span + (4 * i + r), 8, stride=4), :]
                        xp[c, at] = v
                        total = v * v if total is None else total + v * v
                    f = factor(total)
                    fac[at] = f
                    fac_own[at] = f * own[pl.ds(pl.multiple_of(b * per + i, 8), 8)]

    def extended(values, c, m, i):
        down = [values[c, plane(r, i - 1, block)] for r in (m - 2, m - 1)]
        up_ = [values[c, plane(r, i + 1, block)] for r in (0, 1)]
        return down + [values[c, plane(r, i, block)] for r in range(m)] + up_

    def folded(kernel_ref, gain_ref, c):
        return [
            jnp.broadcast_to(kernel_ref[j : j + 1, lanes(c)] * gain_ref[:, lanes(c)], (block, LANES))
            for j in range(5)
        ]

    def taps(c, m, values, factors, gain_ref, kernel_ref, targets, starts):
        k = folded(kernel_ref, gain_ref, c)
        for i in starts:
            f = [factors[plane(r, i - 1, block)] for r in (m - 2, m - 1)]
            f += [factors[plane(r, i, block)] for r in range(m)]
            f += [factors[plane(r, i + 1, block)] for r in (0, 1)]
            ext = [v * w for v, w in zip(extended(values, c, m, i), f)]
            for r in range(m):
                total = k[0] * ext[r]
                for j in range(1, 5):
                    total = total + k[j] * ext[r + j]
                to = slice(r * rows + i, r * rows + i + block)
                targets[0][to, lanes(c)] = total.astype(BF16)
                if len(targets) > 1:
                    if i in edges:
                        total = total * own[i : i + block]
                    targets[1][to, lanes(c)] = total.astype(BF16)

    outer = [b * per + i for b in range(batch) for i in (0, per - 8)]
    inner_blocks = [
        i
        for i in range(block, rows - block, block)
        if not any(i - 1 < j + 8 and i + block >= j for j in outer)
    ]
    outer_blocks = [i for i in range(0, rows, block) if i not in inner_blocks]

    def project_first(starts):
        ranges = []
        for i in starts:
            if ranges and ranges[-1][1] == i:
                ranges[-1][1] = i + block
            else:
                ranges.append([i, i + block])
        size = len(starts) * block
        for k in range(ch // wide):
            for t in range(2):
                part = lanes(k, wide)
                first = [(2 * t + p) * rows for p in range(2)]
                matrix = jnp.concatenate([conv[f + i : f + e] for f in first for i, e in ranges], axis=0)
                pre = jnp.dot(matrix, w1_ref[:, part], preferred_element_type=F32)
                pre = pre + b1_ref[:, part]
                cdf, density = gelu_parts(pre)
                for q in range(wide // LANES):
                    c = k * (wide // LANES) + q
                    offset = 0
                    for i, e in ranges:
                        pooled = None
                        for p in range(2):
                            start = p * size + offset
                            sub = (slice(start, start + e - i), slice(q * LANES, (q + 1) * LANES))
                            slope[c, first[p] + i : first[p] + e] = cdf[sub] + pre[sub] * density[sub]
                            v = xp[c, plane(2 * t + p, i, e - i)] + pre[sub] * cdf[sub]
                            pooled = v if pooled is None else pooled + v
                        up[c, plane(t, i, e - i)] = (pooled * 0.5).astype(BF16).astype(F32)
                        offset += e - i

    def first_section(starts):
        pl.loop(0, groups)(lambda c: taps(c, 4, xp, fac, g1_ref, k1_ref, [conv], starts))
        project_first(starts)

    load_planes(range(8, per - 8, 8))
    loads[2].wait()
    first_section(inner_blocks)

    loads[1].wait()
    for b in range(batch):
        cot[b * per + side : (b + 1) * per - side] = c_ref[b].astype(F32) * 0.5
    for copy in halo:
        copy.wait()

    for b in range(batch):
        base = b * per
        first = cb_ref[b].astype(F32)[HALO - side :] * 0.5
        last = ca_ref[b].astype(F32)[:side] * 0.5
        cot[base : base + side] = jnp.where(at_first, 0.0, first)
        cot[base + per - side : base + per] = jnp.where(at_last, 0.0, last)

    for c in range(groups):
        for b in range(batch):
            base = b * span
            xs[c, base : base + HALO] = jnp.where(at_first, 0.0, xb_ref[b, :, lanes(c)].astype(F32))
            xs[c, base + HALO + length : base + span] = jnp.where(
                at_last, 0.0, xa_ref[b, :, lanes(c)].astype(F32)
            )

    load_planes((0, per - 8))
    first_section(outer_blocks)
    loads[3].wait()

    for c in range(groups):
        for t in range(2):
            for i in edges:
                up[c, plane(t, i, block)] = up[c, plane(t, i, block)] * inside[i : i + block]
            for p in range(2):
                for i in edges:
                    to = slice((2 * t + p) * rows + i, (2 * t + p) * rows + i + block)
                    conv[to, lanes(c)] = (conv[to, lanes(c)].astype(F32) * own[i : i + block]).astype(BF16)

    for t in range(2):
        for i in range(0, rows, block):
            total = None
            for c in range(groups):
                v = up[c, plane(t, i, block)]
                total = v * v if total is None else total + v * v
            f = factor(total)
            fac2[plane(t, i, block)] = f
            fac2_own[plane(t, i, block)] = f * own[i : i + block] if i in edges else f
    pl.loop(0, groups)(lambda c: taps(c, 2, up, fac2, g2_ref, k2_ref, [conv2, conv2_own], range(0, rows, block)))

    nt = (((1,), (1,)), ((), ()))
    tn = (((0,), (0,)), ((), ()))

    if blocks:
        sums = (rest[0:8], rest[8:16])
        srecv1, ssum, srecv2, sall, sfin, sfrecv, small_send, small_recv = rest[16:24]
        small_sems = (small_send, small_recv)
        widths = (-(-ch2 // 256) * LANES, -(-ch // 256) * LANES)
        starts = (ch2 - widths[0], ch - widths[1])

        def small_part(e, who):
            return pl.ds(pl.multiple_of(who * starts[e], LANES), widths[e])

        def small_copies(e):
            w, k = widths[e], 6 * e
            block = pl.ds(8 * e, 8)
            mine = sall.at[e, z, :, pl.ds(0, w)]
            return (
                [(small_ref.at[block], srecv1.at[e], k, mate)],
                [(ssum.at[e, :, small_part(e, core)], srecv2.at[e, :, pl.ds(0, w)], k + 1, over)],
                [(mine, mine, k + 2 + i, at_z(order[i])) for i in range(3)],
                [(sfin.at[e, :, pl.ds(0, w)], sfrecv.at[e, :, pl.ds(0, w)], k + 5, mate)],
            )

        def small_stage(e, stage):
            copies = small_copies(e)
            w = widths[e]
            if stage:
                for source, target, k, other in copies[stage - 1]:
                    remote(source, target, small_sems, k, other).wait()
            if stage == 1:
                ssum[e] = small_ref[8 * e : 8 * e + 8] + srecv1[e]
            if stage == 2:
                sall[e, z, :, 0:w] = ssum[e, :, small_part(e, core)] + srecv2[e, :, 0:w]
            if stage == 3:
                sfin[e, :, 0:w] = (sall[e, 0, :, 0:w] + sall[e, 1, :, 0:w]) + (
                    sall[e, 2, :, 0:w] + sall[e, 3, :, 0:w]
                )
            if stage == 4:
                small_out[8 * e : 8 * e + 8, small_part(e, core)] = sfin[e, :, 0:w]
                small_out[8 * e : 8 * e + 8, small_part(e, 1 - core)] = sfrecv[e, :, 0:w]
                return
            for source, target, k, other in copies[stage]:
                send(source, target, small_sems, k, other)

        def fill(m, zt, term):
            blk = sums[m][0]
            size = blk.shape[3]
            for d in range(4):
                blk[d % 2, zt, d // 2] = term[d * size : (d + 1) * size].astype(BF16)

        def core_copy(m, zt):
            blk, recv1, sems = sums[m][0], sums[m][1], sums[m][6:8]
            return remote(blk.at[1 - core, zt], recv1.at[zt], sems, zt, mate)

        def y_copy(m, zt):
            send2, recv2, sems = sums[m][2], sums[m][3], sums[m][6:8]
            return remote(send2.at[zt], recv2.at[zt], sems, 4 + zt, over)

        def z_copy(m, zt):
            send3, recv3, sems = sums[m][4], sums[m][5], sums[m][6:8]
            return remote(send3.at[zt], recv3.at[z], sems, (8 + zt, 8 + z), at_z(zt))

        def stage_y(m, zt):
            blk, recv1, send2 = sums[m][:3]
            core_copy(m, zt).wait()
            send2[zt] = (blk[core, zt, 1 - y].astype(F32) + recv1[zt, 1 - y].astype(F32)).astype(BF16)
            y_copy(m, zt).start()

        def half_sum(m, zt):
            blk, recv1, recv2 = sums[m][0], sums[m][1], sums[m][3]
            kept = blk[core, zt, y].astype(F32) + recv1[zt, y].astype(F32)
            return kept + recv2[zt].astype(F32)

        def z_send(m, zt):
            sums[m][4][zt] = half_sum(m, zt).astype(BF16)
            z_copy(m, zt).start()

        def stage_z(m, i):
            zt = order[i]
            y_copy(m, zt).wait()
            if i < 3:
                z_send(m, zt)

        def stage_end(m, target):
            recv3, sems = sums[m][5], sums[m][6:8]
            total = half_sum(m, z)
            for zt in order[:3]:
                remote(
                    sums[m][4].at[zt], recv3.at[zt], sems, (8 + zt, 8 + zt), at_z(zt)
                ).wait()
                total = total + recv3[zt].astype(F32)
            target[...] = total

    def own_sum(value):
        total, first = None, 0
        for i in edges + [rows]:
            parts = [value[first:i]] if i > first else []
            if i < rows:
                mask = jnp.concatenate([own[i : i + block]] * (value.shape[1] // LANES), axis=1)
                parts.append(value[i : i + block] * mask)
            for part in parts:
                part = jnp.sum(part, axis=0, keepdims=True)
                total = part if total is None else total + part
            first = i + block
        return total

    quarter = ch2 // 4
    for s in range(0, ch2, wide):
        e = min(s + wide, ch2)
        part = slice(s, e)
        pre = jnp.dot(conv2[...], w2_ref[:, part], preferred_element_type=F32) + b2_ref[:, part]
        cdf, density = gelu_parts(pre)
        grad = cot[:, part]
        total = jnp.zeros((1, e - s), F32)
        for t in range(2):
            at = slice(t * rows, (t + 1) * rows)
            value = grad * (cdf[at] + pre[at] * density[at])
            back2[at, part] = value.astype(BF16)
            total = total + own_sum(value)
        small_ref[6:7, part] = total * scale

    if blocks:
        halves = (1 - z // 2, z // 2)
        over_half = -(-ch2 // 256) * LANES
        skip = ch2 // 2 - (ch2 - over_half)
        for first in halves:
            columns = pl.ds(pl.multiple_of(first * (ch2 - over_half), LANES), over_half)
            gt[0:over_half] = (
                lax.dot_general(
                    back2[:, columns], conv2_own[...], tn, preferred_element_type=F32
                )
                * scale
            )
            for i in range(2):
                zt = 2 * first + i
                start = pl.multiple_of(first * skip + i * quarter, 8)
                fill(1, zt, gt[pl.ds(start, quarter)])
                core_copy(1, zt).start()
    else:
        gt2_ref[...] = (
            lax.dot_general(back2[...], conv2_own[...], tn, preferred_element_type=F32) * scale
        )

    def taps_back(c, m, values, factors, gain_ref, kernel_ref, grads, kernel_row):
        k = folded(kernel_ref, gain_ref, c)
        totals = [None] * 5
        for i in range(0, rows, block):
            ext = extended(grads, c, m, i)
            for r in range(m):
                at = plane(r, i, block)
                v = values[c, at]
                vf = v * factors[at]
                for j in range(5):
                    term = vf * ext[r + 4 - j]
                    totals[j] = term if totals[j] is None else totals[j] + term
                d = k[0] * ext[r + 4]
                for j in range(1, 5):
                    d = d + k[j] * ext[r + 4 - j]
                dn[c, at] = d
                ss[at] += d * v
        for j in range(5):
            small_ref[kernel_row + j : kernel_row + j + 1, lanes(c)] = (
                jnp.sum(totals[j], axis=0, keepdims=True) * gain_ref[:, lanes(c)]
            ) * scale

    def inner(m, factors):
        for r in range(m):
            for i in range(0, rows, block):
                at = plane(r, i, block)
                f = factors[at]
                mean = jnp.sum(ss[at], axis=1, keepdims=True) * (1.0 / ch)
                ss[at] = f * f * f * jnp.broadcast_to(mean, f.shape)

    def scatter(target, result, m, k):
        for q in range(wide // LANES):
            for r in range(m):
                target[k * (wide // LANES) + q, plane(r)] = result[
                    r * rows : (r + 1) * rows, q * LANES : (q + 1) * LANES
                ]

    for k in range(ch // wide):
        scatter(
            into2,
            lax.dot_general(back2[...], w2_ref[lanes(k, wide), :], nt, preferred_element_type=F32),
            2,
            k,
        )
        if blocks and k == 0:
            stage_y(1, order[0])
            stage_y(1, order[1])
        if blocks and k == 1:
            stage_y(1, order[2])
    ss[...] = jnp.zeros_like(ss)

    @pl.loop(0, groups)
    def _(c):
        taps_back(c, 2, up, fac2_own, g2_ref, k2_ref, into2, 0)

    if blocks:
        small_stage(0, 0)
    inner(2, fac2)

    half = ch // 2
    for h in range(2):
        first = halves[h] if blocks else h

        @pl.loop(0, groups // 2)
        def _(step):
            c = first * (groups // 2) + step
            total = None
            for i in range(0, rows, block):
                for t in range(2):
                    at = plane(t, i, block)
                    grad = cot[i : i + block, lanes(c)]
                    d = (fac2[at] * dn[c, at] - up[c, at] * ss[at] + grad) * 0.5
                    if i in edges:
                        d = d * inside[i : i + block]
                    up[c, at] = d
                    for r in (2 * t, 2 * t + 1):
                        to = slice(r * rows + i, r * rows + i + block)
                        value = d * slope[c, to]
                        back[to, lanes(c)] = value.astype(BF16)
                        if i in edges:
                            value = value * own[i : i + block]
                        total = value if total is None else total + value
            small_ref[13:14, lanes(c)] = jnp.sum(total, axis=0, keepdims=True) * scale

        term = (
            lax.dot_general(
                back[:, lanes(first, half)], conv[...], tn, preferred_element_type=F32
            )
            * scale
        )
        if blocks:
            for i in range(2):
                zt = 2 * first + i
                fill(0, zt, term[i * (half // 2) : (i + 1) * (half // 2)])
                core_copy(0, zt).start()
            if h:
                stage_y(0, order[0])
                stage_y(0, order[1])
            else:
                small_stage(0, 1)
            stage_z(1, h)
        else:
            gt1_ref[h * half : (h + 1) * half] = term

    for k in range(ch // wide):
        scatter(
            into,
            lax.dot_general(back[...], w1_ref[lanes(k, wide), :], nt, preferred_element_type=F32),
            4,
            k,
        )

    if blocks:
        stage_y(0, order[2])
        stage_z(1, 2)
    ss[...] = jnp.zeros_like(ss)

    def first_back(c):
        taps_back(c, 4, xp, fac_own, g1_ref, k1_ref, into, 8)

    pl.loop(0, groups // 2)(first_back)
    if blocks:
        small_stage(0, 2)
    pl.loop(groups // 2, groups)(first_back)
    if blocks:
        small_stage(1, 0)
        stage_z(0, 0)
    inner(4, fac)

    def out_copy(c):
        part = lanes(c)
        return pltpu.make_async_copy(fin.at[:, :, part], out_hbm.at[:, :, part], out_sem.at[c])

    def finish(c):
        for i in range(0, rows, block):
            for r in range(4):
                at = plane(r, i, block)
                v = up[c, plane(r // 2, i, block)] + fac[at] * dn[c, at] - xp[c, at] * ss[at]
                mix[pl.ds(4 * i + r, block, stride=4), :] = v
        for b in range(batch):
            base = b * span + HALO
            fin[b, :, lanes(c)] = mix[base : base + length].astype(BF16)
        out_copy(c).start()

    pl.loop(0, groups // 2)(finish)
    if blocks:
        small_stage(1, 1)
        stage_y(1, order[3])
        stage_y(0, order[3])
        stage_z(0, 1)
    pl.loop(groups // 2, groups)(finish)
    if blocks:
        stage_z(0, 2)
        small_stage(1, 2)
        small_stage(0, 3)
        stage_z(1, 3)
        stage_end(1, sum2_ref)
        stage_z(0, 3)
        small_stage(0, 4)
        small_stage(1, 3)
        stage_end(0, sum1_ref)
        small_stage(1, 4)
    else:
        small_out[...] = small_ref[...]
    @pl.loop(0, groups)
    def _(c):
        out_copy(c).wait()


def tail_kernel(fast, p_ref, small_in, gain1_in, k1_in, gain2_in, k2_in, *refs):
    count = 3 if fast else 1
    sources = [p_ref] + list(refs[: count - 1])
    targets, refs = refs[count - 1 : 2 * count - 1], refs[2 * count - 1 :]
    b1_out, b2_out, k1_out, k2_out, g1_out, g2_out = refs[:6]
    held, refs = refs[6 : 6 + count], refs[6 + count :]
    small_ref, gain1_ref, k1_ref, gain2_ref, k2_ref, in_sem, out_sem, few_sem = refs
    few = [
        pltpu.make_async_copy(one, two, few_sem.at[k])
        for k, (one, two) in enumerate(
            zip((small_in, gain1_in, k1_in, gain2_in, k2_in), refs[:5])
        )
    ]
    moves = []
    for source, middle, target in zip(sources, held, targets):
        parts = [(source, middle, target)]
        if not moves:
            length = p_ref.shape[1]
            step = length // 4
            parts = [
                tuple(ref.at[b, pl.ds(s, step)] for ref in parts[0])
                for b in range(p_ref.shape[0])
                for s in range(0, length, step)
            ]
        for one, two, three in parts:
            k = len(moves)
            moves.append(
                (
                    pltpu.make_async_copy(one, two, in_sem.at[k]),
                    pltpu.make_async_copy(two, three, out_sem.at[k]),
                )
            )
    for move in moves:
        move[0].start()
    for copy in few:
        copy.start()
    for move in moves:
        move[0].wait()
        move[1].start()
    for copy in few:
        copy.wait()
    ch = b1_out.shape[0]
    b1_out[...] = small_ref[13, :ch]
    b2_out[...] = small_ref[6, :]
    k1_out[...] = small_ref[8:13, :ch]
    k2_out[...] = small_ref[0:5, :ch]
    for row, k_ref, gain_ref, g_out in ((8, k1_ref, gain1_ref, g1_out), (0, k2_ref, gain2_ref, g2_out)):
        total = jnp.sum(small_ref[row : row + 5, :ch] * k_ref[...], axis=0)
        g_out[...] = total / gain_ref[...]
    for move in moves:
        move[1].wait()


def sums_scratch(ch, ch2, small_shape):
    shapes = []
    for size in (ch // 16, ch2 // 16):
        shapes += [
            pltpu.VMEM((2, 4, 2, size, ch), BF16),
            pltpu.VMEM((4, 2, size, ch), BF16),
            pltpu.VMEM((4, size, ch), BF16),
            pltpu.VMEM((4, size, ch), BF16),
            pltpu.VMEM((4, size, ch), BF16),
            pltpu.VMEM((4, size, ch), BF16),
            pltpu.SemaphoreType.DMA((12,)),
            pltpu.SemaphoreType.DMA((12,)),
        ]
    width = small_shape[1]
    shapes += [pltpu.VMEM((2, 8, width), F32)] * 3 + [pltpu.VMEM((2, 4, 8, width), F32)]
    shapes += [pltpu.VMEM((2, 8, width), F32)] * 2
    return shapes + [pltpu.SemaphoreType.DMA((12,)), pltpu.SemaphoreType.DMA((12,))]


def per_device(fast, n, x, g1, k1, w1, b1, g2, k2, w2, b2, cot):
    batch, length, ch = x.shape
    quarter, ch2 = cot.shape[1:]
    scale = 1.0 / math.sqrt(batch * length * n)
    any_spec = pl.BlockSpec(memory_space=pl.ANY)
    vmem = pl.BlockSpec(memory_space=pltpu.VMEM)

    rows = batch * (length + 2 * HALO) // 4
    small_shape = (16, ch2)
    groups, pitch = ch // LANES, rows + 16
    if fast:
        grads = [jax.ShapeDtypeStruct((k // 16, ch), F32) for k in (ch, ch2)]
    else:
        grads = [jax.ShapeDtypeStruct((ch, ch), F32), jax.ShapeDtypeStruct((ch2, ch), F32)]
    outs = pl.pallas_call(
        functools.partial(step_kernel, scale, n, fast),
        out_shape=[jax.ShapeDtypeStruct(x.shape, BF16)]
        + grads
        + [jax.ShapeDtypeStruct(small_shape, F32)],
        in_specs=[any_spec] + [vmem] * 2 + [any_spec] + [vmem] * 3 + [any_spec, vmem, any_spec],
        out_specs=[any_spec] + [vmem] * (1 + len(grads)),
        scratch_shapes=[
            pltpu.VMEM(x.shape, BF16),
            pltpu.VMEM(cot.shape, BF16),
            pltpu.VMEM((groups, 4 * rows, LANES), F32),
            pltpu.VMEM((groups, 4 * pitch, LANES), F32),
            pltpu.VMEM((4 * pitch, LANES), F32),
            pltpu.VMEM((4 * pitch, LANES), F32),
            pltpu.VMEM((4 * rows, ch), BF16),
            pltpu.VMEM((groups, 4 * rows, LANES), F32),
            pltpu.VMEM((groups, 2 * pitch, LANES), F32),
            pltpu.VMEM((2 * pitch, LANES), F32),
            pltpu.VMEM((2 * pitch, LANES), F32),
            pltpu.VMEM((2 * rows, ch), BF16),
            pltpu.VMEM((2 * rows, ch), BF16),
            pltpu.VMEM((2 * rows, ch2), BF16),
            pltpu.VMEM((groups, 2 * pitch, LANES), F32),
            pltpu.VMEM((rows, ch2), F32),
            pltpu.VMEM((4 * pitch, LANES), F32),
            pltpu.VMEM((rows, LANES), F32),
            pltpu.VMEM((rows, LANES), F32),
            pltpu.VMEM((4 * rows, ch), BF16),
            pltpu.VMEM((groups, 4 * pitch, LANES), F32),
            pltpu.VMEM((groups, 4 * pitch, LANES), F32),
            pltpu.VMEM((ch2, ch), F32),
            pltpu.VMEM((4 * rows, LANES), F32),
            pltpu.VMEM(x.shape, BF16),
            pltpu.VMEM((batch, HALO, ch), BF16),
            pltpu.VMEM((batch, HALO, ch), BF16),
            pltpu.VMEM((batch, HALO, ch2), BF16),
            pltpu.VMEM((batch, HALO, ch2), BF16),
            pltpu.VMEM(w1.shape, BF16),
            pltpu.VMEM(w2.shape, BF16),
            pltpu.VMEM((1, ch), F32),
            pltpu.VMEM((1, ch), F32),
            pltpu.VMEM((1, ch), F32),
            pltpu.VMEM((1, ch2), F32),
            pltpu.VMEM(small_shape, F32),
            pltpu.SemaphoreType.DMA((4,)),
            pltpu.SemaphoreType.DMA((4,)),
            pltpu.SemaphoreType.DMA((4,)),
            pltpu.SemaphoreType.DMA((ch // LANES,)),
        ]
        + (sums_scratch(ch, ch2, small_shape) if fast else []),
        compiler_params=pltpu.CompilerParams(
            collective_id=0, has_side_effects=True, vmem_limit_bytes=60 * 2**20
        ),
        name="step",
    )(x, g1, k1, w1, b1, g2, k2, w2, b2, cot)
    planes, *parts, small = outs
    if not fast:
        grad_w = [
            lax.psum_scatter(part, "seq", scatter_dimension=0, tiled=True).T for part in parts
        ]
        small = lax.psum(small, "seq")
        parts = []

    results = [(ch,), (ch2,), (5, ch), (5, ch), (ch,), (ch,)]
    grad_x, *rest = pl.pallas_call(
        functools.partial(tail_kernel, fast),
        out_shape=[jax.ShapeDtypeStruct(x.shape, BF16)]
        + [jax.ShapeDtypeStruct(part.shape, F32) for part in parts]
        + [jax.ShapeDtypeStruct(shape, F32) for shape in results],
        in_specs=[any_spec] * (6 + len(parts)),
        out_specs=[any_spec] * (1 + len(parts)) + [vmem] * len(results),
        scratch_shapes=[pltpu.VMEM(x.shape, BF16)]
        + [pltpu.VMEM(part.shape, F32) for part in parts]
        + [pltpu.VMEM(arg.shape, F32) for arg in (small, g1, k1, g2, k2)]
        + [pltpu.SemaphoreType.DMA((4 * batch + 2,))] * 2
        + [pltpu.SemaphoreType.DMA((5,))],
        name="tail",
    )(planes, small, g1, k1, g2, k2, *parts)
    if fast:
        grad_w, rest = [part.T for part in rest[:2]], rest[2:]
    return (grad_x, *grad_w, *rest)


def solution(mesh):
    n = mesh.shape["seq"]
    return jax.shard_map(
        functools.partial(per_device, n == 16, n),
        mesh=mesh,
        in_specs=(P("groups", "seq", None),) + (P(),) * 8 + (P("groups", "seq", None),),
        out_specs=(
            P("groups", "seq", None),
            P("groups", "seq"),
            P("groups", "seq"),
            P("groups"),
            P("groups"),
            P("groups", None),
            P("groups", None),
            P("groups"),
            P("groups"),
        ),
        check_vma=False,
    )
```

```python
import functools
import math

import jax
import jax.numpy as jnp
from jax import lax
from jax.experimental import pallas as pl
from jax.experimental.pallas import tpu as pltpu
from jax.sharding import PartitionSpec as P

MESH = pl.DeviceIdType.MESH
F32 = jnp.float32
BF16 = jnp.bfloat16
epsilon = 1e-06
inv_sqrt_two = 0.7071067811865476
inv_sqrt_tau = 0.3989422804014327
HALO = 16
LANES = 128


def gelu_parts(v):
    cdf = 0.5 * (1.0 + lax.erf(v * inv_sqrt_two))
    return cdf, jnp.exp(-0.5 * v * v) * inv_sqrt_tau


def step_kernel(
    scale,
    n,
    blocks,
    x_hbm,
    g1_in,
    k1_ref,
    w1_hbm,
    b1_in,
    g2_in,
    k2_ref,
    w2_hbm,
    b2_in,
    c_hbm,
    out_hbm,
    *rest,
):
    if blocks:
        sum1_ref, sum2_ref, small_out = rest[:3]
    else:
        gt1_ref, gt2_ref, small_out = rest[:3]
    (x_ref, c_ref, xs, xp, fac, fac_own, conv, slope, up, fac2, fac2_own, conv2, conv2_own, back2,
     into2, cot, ss, own, inside, back, into, dn, gt, mix, fin, xb_ref, xa_ref, cb_ref, ca_ref,
     w1_ref, w2_ref, g1_ref, b1_ref, g2_ref, b2_ref, small_ref, halo_send, halo_recv, load_sem,
     out_sem) = rest[3:43]
    rest = rest[43:]
    batch, length, ch = x_ref.shape
    ch2 = c_ref.shape[2]
    span = length + 2 * HALO
    per = span // 4
    rows = batch * per
    groups = ch // LANES
    side = HALO // 4
    wide = 256
    pitch = rows + 16
    block = 16
    edges = [i for i in range(0, rows, block) if any((i + j) % per in (0, per - 1) for j in range(block))]

    def plane(r, i=0, size=None):
        first = r * pitch + 8 + i
        return slice(first, first + (rows if size is None else size))

    me = lax.axis_index("seq")
    right, left = lax.rem(me + 1, n), lax.rem(me + n - 1, n)
    others = [left, right]
    if blocks:
        z, y, core = me // 4, lax.rem(me // 2, 2), lax.rem(me, 2)
        mate, over = me + 1 - 2 * core, me + 2 - 4 * y
        near = z + 1 - 2 * lax.rem(z, 2)
        order = [lax.rem(z + 2, 4), lax.rem(near + 2, 4), near, z]

        def at_z(zt):
            return zt * 4 + y * 2 + core

        others += [mate, over] + [at_z(zt) for zt in order[:3]]
    loads = [
        pltpu.make_async_copy(source, target, load_sem.at[k])
        for k, (source, target) in enumerate(
            ((x_hbm, x_ref), (c_hbm, c_ref), (w1_hbm, w1_ref), (w2_hbm, w2_ref))
        )
    ]
    barrier = pltpu.get_barrier_semaphore()
    for other in others:
        pl.semaphore_signal(barrier, inc=1, device_id={"seq": other}, device_id_type=MESH)
    for load in loads:
        load.start()
    for source, target in ((g1_in, g1_ref), (b1_in, b1_ref), (g2_in, g2_ref), (b2_in, b2_ref)):
        target[...] = source[...].reshape(target.shape)

    within = lax.broadcasted_iota(jnp.int32, (rows, LANES), 0)
    for b in range(1, batch):
        within = jnp.where(within >= per, within - per, within)
    is_own = (within >= side) & (within < per - side)
    own[...] = jnp.where(is_own, 1.0, 0.0)
    at_first, at_last = me == 0, me == n - 1
    low = jnp.where(at_first, side, 0)
    high = jnp.where(at_last, per - side, per)
    inside[...] = jnp.where((within >= low) & (within < high), 1.0, 0.0)
    small_ref[...] = jnp.zeros_like(small_ref)
    for ref, m in ((fac, 4), (fac_own, 4), (fac2, 2), (fac2_own, 2)):
        for r in range(m):
            for i in (-8, rows):
                ref[plane(r, i, 8)] = jnp.zeros((8, LANES), F32)
    for ref, m in ((xp, 4), (into, 4), (up, 2), (into2, 2)):
        for r in range(m):
            for i in (-8, rows):
                ref[:, plane(r, i, 8)] = jnp.zeros((groups, 8, LANES), F32)
    pl.semaphore_wait(barrier, len(others))

    def remote(source, target, sems, k, other):
        if not isinstance(k, tuple):
            k = (k, k)
        return pltpu.make_async_remote_copy(
            src_ref=source,
            dst_ref=target,
            send_sem=sems[0].at[k[0]],
            recv_sem=sems[1].at[k[1]],
            device_id={"seq": other},
            device_id_type=MESH,
        )

    def send(*args):
        copy = remote(*args)
        copy.start()
        return copy

    halo = []
    for ref, before, after in ((x_hbm, xb_ref, xa_ref), (c_hbm, cb_ref, ca_ref)):
        last = ref.shape[1] - HALO
        for source, target, other in (
            (ref.at[:, pl.ds(last, HALO)], before, right),
            (ref.at[:, pl.ds(0, HALO)], after, left),
        ):
            halo.append(send(source, target, (halo_send, halo_recv), len(halo), other))

    def lanes(c, width=LANES):
        if isinstance(c, int):
            return slice(c * width, (c + 1) * width)
        return pl.ds(pl.multiple_of(c * width, width), width)

    loads[0].wait()

    @pl.loop(0, groups)
    def _(c):
        for b in range(batch):
            base = b * span + HALO
            xs[c, base : base + length] = x_ref[b, :, lanes(c)].astype(F32)

    def factor(total):
        return jnp.broadcast_to(
            lax.rsqrt(jnp.sum(total, axis=1, keepdims=True) * (1.0 / ch) + epsilon), total.shape
        )

    def load_planes(starts):
        @pl.loop(0, batch)
        def _(b):
            for i in starts:
                for r in range(4):
                    at = pl.ds(pl.multiple_of(b * per + (r * pitch + 8 + i), 8), 8)
                    total = None
                    for c in range(groups):
                        v = xs[c, pl.ds(b * span + (4 * i + r), 8, stride=4), :]
                        xp[c, at] = v
                        total = v * v if total is None else total + v * v
                    f = factor(total)
                    fac[at] = f
                    fac_own[at] = f * own[pl.ds(pl.multiple_of(b * per + i, 8), 8)]

    def extended(values, c, m, i):
        down = [values[c, plane(r, i - 1, block)] for r in (m - 2, m - 1)]
        up_ = [values[c, plane(r, i + 1, block)] for r in (0, 1)]
        return down + [values[c, plane(r, i, block)] for r in range(m)] + up_

    def folded(kernel_ref, gain_ref, c):
        return [
            jnp.broadcast_to(kernel_ref[j : j + 1, lanes(c)] * gain_ref[:, lanes(c)], (block, LANES))
            for j in range(5)
        ]

    def taps(c, m, values, factors, gain_ref, kernel_ref, targets, starts):
        k = folded(kernel_ref, gain_ref, c)
        for i in starts:
            f = [factors[plane(r, i - 1, block)] for r in (m - 2, m - 1)]
            f += [factors[plane(r, i, block)] for r in range(m)]
            f += [factors[plane(r, i + 1, block)] for r in (0, 1)]
            ext = [v * w for v, w in zip(extended(values, c, m, i), f)]
            for r in range(m):
                total = k[0] * ext[r]
                for j in range(1, 5):
                    total = total + k[j] * ext[r + j]
                to = slice(r * rows + i, r * rows + i + block)
                targets[0][to, lanes(c)] = total.astype(BF16)
                if len(targets) > 1:
                    if i in edges:
                        total = total * own[i : i + block]
                    targets[1][to, lanes(c)] = total.astype(BF16)

    outer = [b * per + i for b in range(batch) for i in (0, per - 8)]
    inner_blocks = [
        i
        for i in range(block, rows - block, block)
        if not any(i - 1 < j + 8 and i + block >= j for j in outer)
    ]
    outer_blocks = [i for i in range(0, rows, block) if i not in inner_blocks]

    def project_first(starts):
        ranges = []
        for i in starts:
            if ranges and ranges[-1][1] == i:
                ranges[-1][1] = i + block
            else:
                ranges.append([i, i + block])
        size = len(starts) * block
        for k in range(ch // wide):
            for t in range(2):
                part = lanes(k, wide)
                first = [(2 * t + p) * rows for p in range(2)]
                matrix = jnp.concatenate([conv[f + i : f + e] for f in first for i, e in ranges], axis=0)
                pre = jnp.dot(matrix, w1_ref[:, part], preferred_element_type=F32)
                pre = pre + b1_ref[:, part]
                cdf, density = gelu_parts(pre)
                for q in range(wide // LANES):
                    c = k * (wide // LANES) + q
                    offset = 0
                    for i, e in ranges:
                        pooled = None
                        for p in range(2):
                            start = p * size + offset
                            sub = (slice(start, start + e - i), slice(q * LANES, (q + 1) * LANES))
                            slope[c, first[p] + i : first[p] + e] = cdf[sub] + pre[sub] * density[sub]
                            v = xp[c, plane(2 * t + p, i, e - i)] + pre[sub] * cdf[sub]
                            pooled = v if pooled is None else pooled + v
                        up[c, plane(t, i, e - i)] = (pooled * 0.5).astype(BF16).astype(F32)
                        offset += e - i

    def first_section(starts):
        pl.loop(0, groups)(lambda c: taps(c, 4, xp, fac, g1_ref, k1_ref, [conv], starts))
        project_first(starts)

    load_planes(range(8, per - 8, 8))
    loads[2].wait()
    first_section(inner_blocks)

    loads[1].wait()
    for b in range(batch):
        cot[b * per + side : (b + 1) * per - side] = c_ref[b].astype(F32) * 0.5
    for copy in halo:
        copy.wait()

    for b in range(batch):
        base = b * per
        first = cb_ref[b].astype(F32)[HALO - side :] * 0.5
        last = ca_ref[b].astype(F32)[:side] * 0.5
        cot[base : base + side] = jnp.where(at_first, 0.0, first)
        cot[base + per - side : base + per] = jnp.where(at_last, 0.0, last)

    for c in range(groups):
        for b in range(batch):
            base = b * span
            xs[c, base : base + HALO] = jnp.where(at_first, 0.0, xb_ref[b, :, lanes(c)].astype(F32))
            xs[c, base + HALO + length : base + span] = jnp.where(
                at_last, 0.0, xa_ref[b, :, lanes(c)].astype(F32)
            )

    load_planes((0, per - 8))
    first_section(outer_blocks)
    loads[3].wait()

    for c in range(groups):
        for t in range(2):
            for i in edges:
                up[c, plane(t, i, block)] = up[c, plane(t, i, block)] * inside[i : i + block]
            for p in range(2):
                for i in edges:
                    to = slice((2 * t + p) * rows + i, (2 * t + p) * rows + i + block)
                    conv[to, lanes(c)] = (conv[to, lanes(c)].astype(F32) * own[i : i + block]).astype(BF16)

    for t in range(2):
        for i in range(0, rows, block):
            total = None
            for c in range(groups):
                v = up[c, plane(t, i, block)]
                total = v * v if total is None else total + v * v
            f = factor(total)
            fac2[plane(t, i, block)] = f
            fac2_own[plane(t, i, block)] = f * own[i : i + block] if i in edges else f
    pl.loop(0, groups)(lambda c: taps(c, 2, up, fac2, g2_ref, k2_ref, [conv2, conv2_own], range(0, rows, block)))

    nt = (((1,), (1,)), ((), ()))
    tn = (((0,), (0,)), ((), ()))

    if blocks:
        sums = (rest[0:8], rest[8:16])
        srecv1, ssum, srecv2, sall, sfin, sfrecv, small_send, small_recv = rest[16:24]
        small_sems = (small_send, small_recv)
        widths = (-(-ch2 // 256) * LANES, -(-ch // 256) * LANES)
        starts = (ch2 - widths[0], ch - widths[1])

        def small_part(e, who):
            return pl.ds(pl.multiple_of(who * starts[e], LANES), widths[e])

        def small_copies(e):
            w, k = widths[e], 6 * e
            block = pl.ds(8 * e, 8)
            mine = sall.at[e, z, :, pl.ds(0, w)]
            return (
                [(small_ref.at[block], srecv1.at[e], k, mate)],
                [(ssum.at[e, :, small_part(e, core)], srecv2.at[e, :, pl.ds(0, w)], k + 1, over)],
                [(mine, mine, k + 2 + i, at_z(order[i])) for i in range(3)],
                [(sfin.at[e, :, pl.ds(0, w)], sfrecv.at[e, :, pl.ds(0, w)], k + 5, mate)],
            )

        def small_stage(e, stage):
            copies = small_copies(e)
            w = widths[e]
            if stage:
                for source, target, k, other in copies[stage - 1]:
                    remote(source, target, small_sems, k, other).wait()
            if stage == 1:
                ssum[e] = small_ref[8 * e : 8 * e + 8] + srecv1[e]
            if stage == 2:
                sall[e, z, :, 0:w] = ssum[e, :, small_part(e, core)] + srecv2[e, :, 0:w]
            if stage == 3:
                sfin[e, :, 0:w] = (sall[e, 0, :, 0:w] + sall[e, 1, :, 0:w]) + (
                    sall[e, 2, :, 0:w] + sall[e, 3, :, 0:w]
                )
            if stage == 4:
                small_out[8 * e : 8 * e + 8, small_part(e, core)] = sfin[e, :, 0:w]
                small_out[8 * e : 8 * e + 8, small_part(e, 1 - core)] = sfrecv[e, :, 0:w]
                return
            for source, target, k, other in copies[stage]:
                send(source, target, small_sems, k, other)

        def fill(m, zt, term):
            blk = sums[m][0]
            size = blk.shape[3]
            for d in range(4):
                blk[d % 2, zt, d // 2] = term[d * size : (d + 1) * size].astype(BF16)

        def core_copy(m, zt):
            blk, recv1, sems = sums[m][0], sums[m][1], sums[m][6:8]
            return remote(blk.at[1 - core, zt], recv1.at[zt], sems, zt, mate)

        def y_copy(m, zt):
            send2, recv2, sems = sums[m][2], sums[m][3], sums[m][6:8]
            return remote(send2.at[zt], recv2.at[zt], sems, 4 + zt, over)

        def z_copy(m, zt):
            send3, recv3, sems = sums[m][4], sums[m][5], sums[m][6:8]
            return remote(send3.at[zt], recv3.at[z], sems, (8 + zt, 8 + z), at_z(zt))

        def stage_y(m, zt):
            blk, recv1, send2 = sums[m][:3]
            core_copy(m, zt).wait()
            send2[zt] = (blk[core, zt, 1 - y].astype(F32) + recv1[zt, 1 - y].astype(F32)).astype(BF16)
            y_copy(m, zt).start()

        def half_sum(m, zt):
            blk, recv1, recv2 = sums[m][0], sums[m][1], sums[m][3]
            kept = blk[core, zt, y].astype(F32) + recv1[zt, y].astype(F32)
            return kept + recv2[zt].astype(F32)

        def z_send(m, zt):
            sums[m][4][zt] = half_sum(m, zt).astype(BF16)
            z_copy(m, zt).start()

        def stage_z(m, i):
            zt = order[i]
            y_copy(m, zt).wait()
            if i < 3:
                z_send(m, zt)

        def stage_end(m, target):
            recv3, sems = sums[m][5], sums[m][6:8]
            total = half_sum(m, z)
            for zt in order[:3]:
                remote(
                    sums[m][4].at[zt], recv3.at[zt], sems, (8 + zt, 8 + zt), at_z(zt)
                ).wait()
                total = total + recv3[zt].astype(F32)
            target[...] = total

    def own_sum(value):
        total, first = None, 0
        for i in edges + [rows]:
            parts = [value[first:i]] if i > first else []
            if i < rows:
                mask = jnp.concatenate([own[i : i + block]] * (value.shape[1] // LANES), axis=1)
                parts.append(value[i : i + block] * mask)
            for part in parts:
                part = jnp.sum(part, axis=0, keepdims=True)
                total = part if total is None else total + part
            first = i + block
        return total

    quarter = ch2 // 4
    for s in range(0, ch2, wide):
        e = min(s + wide, ch2)
        part = slice(s, e)
        pre = jnp.dot(conv2[...], w2_ref[:, part], preferred_element_type=F32) + b2_ref[:, part]
        cdf, density = gelu_parts(pre)
        grad = cot[:, part]
        total = jnp.zeros((1, e - s), F32)
        for t in range(2):
            at = slice(t * rows, (t + 1) * rows)
            value = grad * (cdf[at] + pre[at] * density[at])
            back2[at, part] = value.astype(BF16)
            total = total + own_sum(value)
        small_ref[6:7, part] = total * scale

    if blocks:
        halves = (1 - z // 2, z // 2)
        over_half = -(-ch2 // 256) * LANES
        skip = ch2 // 2 - (ch2 - over_half)
        for first in halves:
            columns = pl.ds(pl.multiple_of(first * (ch2 - over_half), LANES), over_half)
            gt[0:over_half] = (
                lax.dot_general(
                    back2[:, columns], conv2_own[...], tn, preferred_element_type=F32
                )
                * scale
            )
            for i in range(2):
                zt = 2 * first + i
                start = pl.multiple_of(first * skip + i * quarter, 8)
                fill(1, zt, gt[pl.ds(start, quarter)])
                core_copy(1, zt).start()
    else:
        gt2_ref[...] = (
            lax.dot_general(back2[...], conv2_own[...], tn, preferred_element_type=F32) * scale
        )

    def taps_back(c, m, values, factors, gain_ref, kernel_ref, grads, kernel_row):
        k = folded(kernel_ref, gain_ref, c)
        totals = [None] * 5
        for i in range(0, rows, block):
            ext = extended(grads, c, m, i)
            for r in range(m):
                at = plane(r, i, block)
                v = values[c, at]
                vf = v * factors[at]
                for j in range(5):
                    term = vf * ext[r + 4 - j]
                    totals[j] = term if totals[j] is None else totals[j] + term
                d = k[0] * ext[r + 4]
                for j in range(1, 5):
                    d = d + k[j] * ext[r + 4 - j]
                dn[c, at] = d
                ss[at] += d * v
        for j in range(5):
            small_ref[kernel_row + j : kernel_row + j + 1, lanes(c)] = (
                jnp.sum(totals[j], axis=0, keepdims=True) * gain_ref[:, lanes(c)]
            ) * scale

    def inner(m, factors):
        for r in range(m):
            for i in range(0, rows, block):
                at = plane(r, i, block)
                f = factors[at]
                mean = jnp.sum(ss[at], axis=1, keepdims=True) * (1.0 / ch)
                ss[at] = f * f * f * jnp.broadcast_to(mean, f.shape)

    def scatter(target, result, m, k):
        for q in range(wide // LANES):
            for r in range(m):
                target[k * (wide // LANES) + q, plane(r)] = result[
                    r * rows : (r + 1) * rows, q * LANES : (q + 1) * LANES
                ]

    for k in range(ch // wide):
        scatter(
            into2,
            lax.dot_general(back2[...], w2_ref[lanes(k, wide), :], nt, preferred_element_type=F32),
            2,
            k,
        )
        if blocks and k == 0:
            stage_y(1, order[0])
            stage_y(1, order[1])
        if blocks and k == 1:
            stage_y(1, order[2])
    ss[...] = jnp.zeros_like(ss)

    @pl.loop(0, groups)
    def _(c):
        taps_back(c, 2, up, fac2_own, g2_ref, k2_ref, into2, 0)

    if blocks:
        small_stage(0, 0)
    inner(2, fac2)

    half = ch // 2
    for h in range(2):
        first = halves[h] if blocks else h

        @pl.loop(0, groups // 2)
        def _(step):
            c = first * (groups // 2) + step
            total = None
            for i in range(0, rows, block):
                for t in range(2):
                    at = plane(t, i, block)
                    grad = cot[i : i + block, lanes(c)]
                    d = (fac2[at] * dn[c, at] - up[c, at] * ss[at] + grad) * 0.5
                    if i in edges:
                        d = d * inside[i : i + block]
                    up[c, at] = d
                    for r in (2 * t, 2 * t + 1):
                        to = slice(r * rows + i, r * rows + i + block)
                        value = d * slope[c, to]
                        back[to, lanes(c)] = value.astype(BF16)
                        if i in edges:
                            value = value * own[i : i + block]
                        total = value if total is None else total + value
            small_ref[13:14, lanes(c)] = jnp.sum(total, axis=0, keepdims=True) * scale

        term = (
            lax.dot_general(
                back[:, lanes(first, half)], conv[...], tn, preferred_element_type=F32
            )
            * scale
        )
        if blocks:
            for i in range(2):
                zt = 2 * first + i
                fill(0, zt, term[i * (half // 2) : (i + 1) * (half // 2)])
                core_copy(0, zt).start()
            if h:
                stage_y(0, order[0])
                stage_y(0, order[1])
            else:
                small_stage(0, 1)
            stage_z(1, h)
        else:
            gt1_ref[h * half : (h + 1) * half] = term

    for k in range(ch // wide):
        scatter(
            into,
            lax.dot_general(back[...], w1_ref[lanes(k, wide), :], nt, preferred_element_type=F32),
            4,
            k,
        )

    if blocks:
        stage_y(0, order[2])
        stage_z(1, 2)
    ss[...] = jnp.zeros_like(ss)

    def first_back(c):
        taps_back(c, 4, xp, fac_own, g1_ref, k1_ref, into, 8)

    pl.loop(0, groups // 2)(first_back)
    if blocks:
        small_stage(0, 2)
    pl.loop(groups // 2, groups)(first_back)
    if blocks:
        small_stage(1, 0)
        stage_z(0, 0)
    inner(4, fac)

    def out_copy(c):
        part = lanes(c)
        return pltpu.make_async_copy(fin.at[:, :, part], out_hbm.at[:, :, part], out_sem.at[c])

    def finish(c):
        for i in range(0, rows, block):
            for r in range(4):
                at = plane(r, i, block)
                v = up[c, plane(r // 2, i, block)] + fac[at] * dn[c, at] - xp[c, at] * ss[at]
                mix[pl.ds(4 * i + r, block, stride=4), :] = v
        for b in range(batch):
            base = b * span + HALO
            fin[b, :, lanes(c)] = mix[base : base + length].astype(BF16)
        out_copy(c).start()

    pl.loop(0, groups // 2)(finish)
    if blocks:
        small_stage(1, 1)
        stage_y(1, order[3])
        stage_y(0, order[3])
        stage_z(0, 1)
    pl.loop(groups // 2, groups)(finish)
    if blocks:
        stage_z(0, 2)
        small_stage(1, 2)
        small_stage(0, 3)
        stage_z(1, 3)
        stage_end(1, sum2_ref)
        stage_z(0, 3)
        small_stage(0, 4)
        small_stage(1, 3)
        stage_end(0, sum1_ref)
        small_stage(1, 4)
    else:
        small_out[...] = small_ref[...]
    @pl.loop(0, groups)
    def _(c):
        out_copy(c).wait()


def tail_kernel(fast, p_ref, small_in, gain1_in, k1_in, gain2_in, k2_in, *refs):
    count = 3 if fast else 1
    sources = [p_ref] + list(refs[: count - 1])
    targets, refs = refs[count - 1 : 2 * count - 1], refs[2 * count - 1 :]
    results = refs[:6]
    held, refs = refs[6 : 6 + count], refs[6 + count :]
    small_ref, gain1_ref, k1_ref, gain2_ref, k2_ref = refs[:5]
    b1_out, b2_out, k1_out, k2_out, g1_out, g2_out = refs[5:11]
    in_sem, out_sem, few_sem = refs[11:]
    ends = [
        pltpu.make_async_copy(one, two, few_sem.at[5 + k])
        for k, (one, two) in enumerate(zip(refs[5:11], results))
    ]
    few = [
        pltpu.make_async_copy(one, two, few_sem.at[k])
        for k, (one, two) in enumerate(
            zip((small_in, gain1_in, k1_in, gain2_in, k2_in), refs[:5])
        )
    ]
    moves = []
    for source, middle, target in zip(sources, held, targets):
        parts = [(source, middle, target)]
        if not moves:
            length = p_ref.shape[1]
            step = length // 4
            parts = [
                tuple(ref.at[b, pl.ds(s, step)] for ref in parts[0])
                for b in range(p_ref.shape[0])
                for s in range(0, length, step)
            ]
        for one, two, three in parts:
            k = len(moves)
            moves.append(
                (
                    pltpu.make_async_copy(one, two, in_sem.at[k]),
                    pltpu.make_async_copy(two, three, out_sem.at[k]),
                )
            )
    for move in moves:
        move[0].start()
    for copy in few:
        copy.start()
    for move in moves:
        move[0].wait()
        move[1].start()
    for copy in few:
        copy.wait()
    ch = b1_out.shape[0]
    b1_out[...] = small_ref[13, :ch]
    b2_out[...] = small_ref[6, :]
    k1_out[...] = small_ref[8:13, :ch]
    k2_out[...] = small_ref[0:5, :ch]
    for row, k_ref, gain_ref, g_out in ((8, k1_ref, gain1_ref, g1_out), (0, k2_ref, gain2_ref, g2_out)):
        total = jnp.sum(small_ref[row : row + 5, :ch] * k_ref[...], axis=0)
        g_out[...] = total / gain_ref[...]
    for copy in ends:
        copy.start()
    for move in moves:
        move[1].wait()
    for copy in ends:
        copy.wait()


def sums_scratch(ch, ch2, small_shape):
    shapes = []
    for size in (ch // 16, ch2 // 16):
        shapes += [
            pltpu.VMEM((2, 4, 2, size, ch), BF16),
            pltpu.VMEM((4, 2, size, ch), BF16),
            pltpu.VMEM((4, size, ch), BF16),
            pltpu.VMEM((4, size, ch), BF16),
            pltpu.VMEM((4, size, ch), BF16),
            pltpu.VMEM((4, size, ch), BF16),
            pltpu.SemaphoreType.DMA((12,)),
            pltpu.SemaphoreType.DMA((12,)),
        ]
    width = small_shape[1]
    shapes += [pltpu.VMEM((2, 8, width), F32)] * 3 + [pltpu.VMEM((2, 4, 8, width), F32)]
    shapes += [pltpu.VMEM((2, 8, width), F32)] * 2
    return shapes + [pltpu.SemaphoreType.DMA((12,)), pltpu.SemaphoreType.DMA((12,))]


def per_device(fast, n, x, g1, k1, w1, b1, g2, k2, w2, b2, cot):
    batch, length, ch = x.shape
    quarter, ch2 = cot.shape[1:]
    scale = 1.0 / math.sqrt(batch * length * n)
    any_spec = pl.BlockSpec(memory_space=pl.ANY)
    vmem = pl.BlockSpec(memory_space=pltpu.VMEM)

    rows = batch * (length + 2 * HALO) // 4
    small_shape = (16, ch2)
    groups, pitch = ch // LANES, rows + 16
    if fast:
        grads = [jax.ShapeDtypeStruct((k // 16, ch), F32) for k in (ch, ch2)]
    else:
        grads = [jax.ShapeDtypeStruct((ch, ch), F32), jax.ShapeDtypeStruct((ch2, ch), F32)]
    outs = pl.pallas_call(
        functools.partial(step_kernel, scale, n, fast),
        out_shape=[jax.ShapeDtypeStruct(x.shape, BF16)]
        + grads
        + [jax.ShapeDtypeStruct(small_shape, F32)],
        in_specs=[any_spec] + [vmem] * 2 + [any_spec] + [vmem] * 3 + [any_spec, vmem, any_spec],
        out_specs=[any_spec] + [vmem] * (1 + len(grads)),
        scratch_shapes=[
            pltpu.VMEM(x.shape, BF16),
            pltpu.VMEM(cot.shape, BF16),
            pltpu.VMEM((groups, 4 * rows, LANES), F32),
            pltpu.VMEM((groups, 4 * pitch, LANES), F32),
            pltpu.VMEM((4 * pitch, LANES), F32),
            pltpu.VMEM((4 * pitch, LANES), F32),
            pltpu.VMEM((4 * rows, ch), BF16),
            pltpu.VMEM((groups, 4 * rows, LANES), F32),
            pltpu.VMEM((groups, 2 * pitch, LANES), F32),
            pltpu.VMEM((2 * pitch, LANES), F32),
            pltpu.VMEM((2 * pitch, LANES), F32),
            pltpu.VMEM((2 * rows, ch), BF16),
            pltpu.VMEM((2 * rows, ch), BF16),
            pltpu.VMEM((2 * rows, ch2), BF16),
            pltpu.VMEM((groups, 2 * pitch, LANES), F32),
            pltpu.VMEM((rows, ch2), F32),
            pltpu.VMEM((4 * pitch, LANES), F32),
            pltpu.VMEM((rows, LANES), F32),
            pltpu.VMEM((rows, LANES), F32),
            pltpu.VMEM((4 * rows, ch), BF16),
            pltpu.VMEM((groups, 4 * pitch, LANES), F32),
            pltpu.VMEM((groups, 4 * pitch, LANES), F32),
            pltpu.VMEM((ch2, ch), F32),
            pltpu.VMEM((4 * rows, LANES), F32),
            pltpu.VMEM(x.shape, BF16),
            pltpu.VMEM((batch, HALO, ch), BF16),
            pltpu.VMEM((batch, HALO, ch), BF16),
            pltpu.VMEM((batch, HALO, ch2), BF16),
            pltpu.VMEM((batch, HALO, ch2), BF16),
            pltpu.VMEM(w1.shape, BF16),
            pltpu.VMEM(w2.shape, BF16),
            pltpu.VMEM((1, ch), F32),
            pltpu.VMEM((1, ch), F32),
            pltpu.VMEM((1, ch), F32),
            pltpu.VMEM((1, ch2), F32),
            pltpu.VMEM(small_shape, F32),
            pltpu.SemaphoreType.DMA((4,)),
            pltpu.SemaphoreType.DMA((4,)),
            pltpu.SemaphoreType.DMA((4,)),
            pltpu.SemaphoreType.DMA((ch // LANES,)),
        ]
        + (sums_scratch(ch, ch2, small_shape) if fast else []),
        compiler_params=pltpu.CompilerParams(
            collective_id=0, has_side_effects=True, vmem_limit_bytes=60 * 2**20
        ),
        name="step",
    )(x, g1, k1, w1, b1, g2, k2, w2, b2, cot)
    planes, *parts, small = outs
    if not fast:
        grad_w = [
            lax.psum_scatter(part, "seq", scatter_dimension=0, tiled=True).T for part in parts
        ]
        small = lax.psum(small, "seq")
        parts = []

    results = [(ch,), (ch2,), (5, ch), (5, ch), (ch,), (ch,)]
    grad_x, *rest = pl.pallas_call(
        functools.partial(tail_kernel, fast),
        out_shape=[jax.ShapeDtypeStruct(x.shape, BF16)]
        + [jax.ShapeDtypeStruct(part.shape, F32) for part in parts]
        + [jax.ShapeDtypeStruct(shape, F32) for shape in results],
        in_specs=[any_spec] * (6 + len(parts)),
        out_specs=[any_spec] * (1 + len(parts) + len(results)),
        scratch_shapes=[pltpu.VMEM(x.shape, BF16)]
        + [pltpu.VMEM(part.shape, F32) for part in parts]
        + [pltpu.VMEM(arg.shape, F32) for arg in (small, g1, k1, g2, k2)]
        + [pltpu.VMEM(shape, F32) for shape in results]
        + [pltpu.SemaphoreType.DMA((4 * batch + 2,))] * 2
        + [pltpu.SemaphoreType.DMA((11,))],
        name="tail",
    )(planes, small, g1, k1, g2, k2, *parts)
    if fast:
        grad_w, rest = [part.T for part in rest[:2]], rest[2:]
    return (grad_x, *grad_w, *rest)


def solution(mesh):
    n = mesh.shape["seq"]
    return jax.shard_map(
        functools.partial(per_device, n == 16, n),
        mesh=mesh,
        in_specs=(P("groups", "seq", None),) + (P(),) * 8 + (P("groups", "seq", None),),
        out_specs=(
            P("groups", "seq", None),
            P("groups", "seq"),
            P("groups", "seq"),
            P("groups"),
            P("groups"),
            P("groups", None),
            P("groups", None),
            P("groups"),
            P("groups"),
        ),
        check_vma=False,
    )
```
